256 devices in a mesh: ta: 64 (over x, y, z_lo, core), gz: 4 (over z_hi).
Axes of the slice: x: 4, y: 4, z: 8 (z_hi: 4, z_lo: 2; z = z_hi * 2 + z_lo), core: 2. Of those that a mesh axis runs over, the one named last changes fastest.
Arguments:
- links: float32 [4, 18, 4, 512, 256], P(None, None, 'gz', 'ta'), may hold values from -1 to 1, as said below
- source: float32 [24, 4, 512, 256], P(None, 'gz', 'ta'), may hold values from -6 to 6
Outputs:
- solution: float32 [24, 4, 512, 256], P(None, 'gz', 'ta')
- residual: float32 [24, 4, 512, 256], P(None, 'gz', 'ta')
The draws below stay inside these ranges and needn't reach their ends.
Inputs may be any that keep to these rules, and one draw needn't show every extreme that they name: `links`: every link is a unitary 3x3 complex matrix.
All inputs are finite; a program needn't handle non-finite values.
Results may differ from the reference program's by a relative error of at most 0.00027.
Values sent between devices are 32-bit elements; how exact they have to be, the bound alone decides.
No kernel may reach another device: no remote copies, remote signals or barrier semaphores. Data moves between devices by JAX's collectives and lax.ppermute only.
A program may use at most 256 MiB of HBM per device.

```python
import jax
import jax.numpy as jnp
from jax import lax

LX = 16
LY = 16
CT = 8
CZ = 1
NMR = 4
NZ = 4
NT = 512
N_TA = 64
N_GZ = 4


def draw_links(key, part):
    plane_sites = LX * LY
    noise = jax.random.normal(key, (2, 3, 3, 4, NZ, NT, plane_sites), jnp.float32)
    matrix_real = noise[0]
    matrix_imag = noise[1]
    rows_real = []
    rows_imag = []
    for row_index in range(3):
        vector_real = matrix_real[row_index]
        vector_imag = matrix_imag[row_index]
        for earlier in range(row_index):
            prior_real = rows_real[earlier]
            prior_imag = rows_imag[earlier]
            project_real = jnp.sum(prior_real * vector_real + prior_imag * vector_imag, axis=0)
            project_imag = jnp.sum(prior_real * vector_imag - prior_imag * vector_real, axis=0)
            vector_real = vector_real - (project_real * prior_real - project_imag * prior_imag)
            vector_imag = vector_imag - (project_real * prior_imag + project_imag * prior_real)
        squared_length = jnp.sum(vector_real * vector_real + vector_imag * vector_imag, axis=0)
        inverse_length = lax.rsqrt(jnp.maximum(squared_length, 1e-12))
        rows_real.append(vector_real * inverse_length)
        rows_imag.append(vector_imag * inverse_length)
    unitary = jnp.stack([jnp.stack(rows_real), jnp.stack(rows_imag)])
    return jnp.transpose(unitary, (3, 0, 1, 2, 4, 5, 6)).reshape((4, 18, NZ, NT, plane_sites))


def level_of(key, dims, split, smallest, top_value):
    loudness = 1.0
    for dim, parts in split:
        heights = jax.random.uniform(jax.random.fold_in(jax.random.fold_in(key, 6), dim), (parts,), jnp.float32, smallest / len(split), top_value / len(split))
        loudness = loudness * jnp.repeat(jnp.exp(heights), dims[dim] // parts).reshape((-1,) + (1,) * (len(dims) - 1 - dim))
    return loudness


def normal_values(key, extent, width, most, split=(), kind=jnp.bfloat16):
    values = jax.random.normal(key, extent, jnp.float32) * width
    if len(split) > 0:
        values = level_of(key, extent, split, -0.22, 0.18) * values
    return jnp.clip(values, min=-most, max=most).astype(kind)


def setup_inputs(seed: int = 0) -> dict:
    key_of = jax.random.split(jax.random.key(seed), 3)
    links = draw_links(jax.random.fold_in(key_of[2], 71), 0)
    source = normal_values(key_of[1], (24, NZ, NT, LY * LX), 1.0, 6.0, ((1, 4), (2, 64)), jnp.float32)
    return {"links": links, "source": source}


bare_mass = 0.2
mean_epsilon = 1e-6
gamma_column = ((3, 2, 1, 0), (3, 2, 1, 0), (2, 3, 0, 1), (2, 3, 0, 1))
gamma_real = ((0, 0, 0, 0), (-1, 1, 1, -1), (0, 0, 0, 0), (1, 1, 1, 1))
gamma_imag = ((1, 1, -1, -1), (0, 0, 0, 0), (1, -1, -1, 1), (0, 0, 0, 0))


def spin_project(field, direction, orientation):
    trailing = field.shape[1:]
    spin_real = field[:12].reshape((4, 3) + trailing)
    spin_imag = field[12:].reshape((4, 3) + trailing)
    rows_real = []
    rows_imag = []
    for spin_row in range(4):
        source_row = gamma_column[direction][spin_row]
        coef_real = orientation * gamma_real[direction][spin_row]
        coef_imag = orientation * gamma_imag[direction][spin_row]
        if coef_real != 0:
            rows_real.append(spin_real[spin_row] + coef_real * spin_real[source_row])
            rows_imag.append(spin_imag[spin_row] + coef_real * spin_imag[source_row])
        else:
            rows_real.append(spin_real[spin_row] - coef_imag * spin_imag[source_row])
            rows_imag.append(spin_imag[spin_row] + coef_imag * spin_real[source_row])
    return jnp.concatenate([jnp.stack(rows_real).reshape((12,) + trailing), jnp.stack(rows_imag).reshape((12,) + trailing)], 0)


def color_apply(link, field, adjoint):
    trailing = field.shape[1:]
    link_real = link[:9].reshape((3, 3) + trailing)
    link_imag = link[9:].reshape((3, 3) + trailing)
    spin_real = field[:12].reshape((4, 3) + trailing)
    spin_imag = field[12:].reshape((4, 3) + trailing)
    out_real = []
    out_imag = []
    for out_color in range(3):
        total_real = None
        total_imag = None
        for in_color in range(3):
            if adjoint:
                entry_real = link_real[in_color, out_color]
                entry_imag = -link_imag[in_color, out_color]
            else:
                entry_real = link_real[out_color, in_color]
                entry_imag = link_imag[out_color, in_color]
            piece_real = entry_real * spin_real[:, in_color] - entry_imag * spin_imag[:, in_color]
            piece_imag = entry_real * spin_imag[:, in_color] + entry_imag * spin_real[:, in_color]
            total_real = piece_real if total_real is None else total_real + piece_real
            total_imag = piece_imag if total_imag is None else total_imag + piece_imag
        out_real.append(total_real)
        out_imag.append(total_imag)
    return jnp.concatenate([jnp.stack(out_real, 1).reshape((12,) + trailing), jnp.stack(out_imag, 1).reshape((12,) + trailing)], 0)


def dirac_terms(field, forward, backward, back_links, links):
    hopping = None
    for direction in range(4):
        contribution = spin_project(color_apply(links[direction], forward[direction], False), direction, -1.0)
        contribution = contribution + spin_project(color_apply(back_links[direction], backward[direction], True), direction, 1.0)
        hopping = contribution if hopping is None else hopping + contribution
    return (4.0 + bare_mass) * field - 0.5 * hopping


def displaced(field, direction, stride):
    if direction < 2:
        lattice_view = field.reshape(field.shape[:3] + (LY, LX))
        which_axis = 4 if direction == 0 else 3
        return jnp.roll(lattice_view, -stride, axis=which_axis).reshape(field.shape)
    return jnp.roll(field, -stride, axis=1 if direction == 2 else 2)


def full_operator(field, links):
    forward = [displaced(field, direction, 1) for direction in range(4)]
    backward = [displaced(field, direction, -1) for direction in range(4)]
    back_links = [displaced(links[direction], direction, -1) for direction in range(4)]
    return dirac_terms(field, forward, backward, back_links, links)


def edge_masks():
    plane = jnp.arange(LY * LX)
    coords = [plane % LX, plane // LX, jnp.arange(NZ), jnp.arange(NT)]
    extents = [LX // 2, LY // 2, CZ, CT]
    shapes = [(1, 1, 1, LY * LX), (1, 1, 1, LY * LX), (1, NZ, 1, 1), (1, 1, NT, 1)]
    ahead = []
    behind = []
    for direction in range(4):
        inner = coords[direction] % extents[direction]
        ahead.append((inner != extents[direction] - 1).astype(jnp.float32).reshape(shapes[direction]))
        behind.append((inner != 0).astype(jnp.float32).reshape(shapes[direction]))
    return ahead, behind


def block_operator(field, links, ahead, behind):
    forward = [displaced(field, direction, 1) * ahead[direction] for direction in range(4)]
    backward = [displaced(field, direction, -1) * behind[direction] for direction in range(4)]
    back_links = [displaced(links[direction], direction, -1) for direction in range(4)]
    return dirac_terms(field, forward, backward, back_links, links)


def block_sum(values):
    shaped = values.reshape((values.shape[0], N_GZ, CZ, N_TA, CT, 2, LY // 2, 2, LX // 2))
    return jnp.sum(shaped, axis=(0, 2, 4, 6, 8))


def spread(per_block):
    wide = jnp.broadcast_to(per_block[None, :, None, :, None, :, None, :, None], (1, N_GZ, CZ, N_TA, CT, 2, LY // 2, 2, LX // 2))
    return wide.reshape((1, NZ, NT, LY * LX))


def complex_scale(weight_real, weight_imag, field):
    scaled_real = weight_real * field[:12] - weight_imag * field[12:]
    scaled_imag = weight_real * field[12:] + weight_imag * field[:12]
    return jnp.concatenate([scaled_real, scaled_imag], 0)


def block_solve(residual, links, ahead, behind, active):
    remainder = residual * active
    update = jnp.zeros_like(residual)
    entries = 12 * (LX // 2) * (LY // 2) * CZ * CT
    for sweep in range(NMR):
        applied = block_operator(remainder, links, ahead, behind)
        margin_real = block_sum(applied[:12] * remainder[:12] + applied[12:] * remainder[12:]) / entries
        margin_imag = block_sum(applied[:12] * remainder[12:] - applied[12:] * remainder[:12]) / entries
        denominator = block_sum(applied * applied) / entries + mean_epsilon
        weight_real = spread(margin_real / denominator)
        weight_imag = spread(margin_imag / denominator)
        update = update + complex_scale(weight_real, weight_imag, remainder)
        remainder = remainder - complex_scale(weight_real, weight_imag, applied)
    return update


def schwarz_cycle(solution, source, links, ahead, behind):
    parity_table = (jnp.arange(N_GZ)[:, None, None, None] + jnp.arange(N_TA)[None, :, None, None] + jnp.arange(2)[None, None, :, None] + jnp.arange(2)[None, None, None, :]) % 2
    for colour in range(2):
        residual = source - full_operator(solution, links)
        active = spread((parity_table == colour).astype(jnp.float32))
        solution = solution + block_solve(residual, links, ahead, behind, active)
    return solution


def reference(links, source):
    ahead, behind = edge_masks()
    solution = schwarz_cycle(jnp.zeros_like(source), source, links, ahead, behind)
    half_block = CT // 2
    moved = schwarz_cycle(jnp.roll(solution, half_block, axis=2), jnp.roll(source, half_block, axis=2), jnp.roll(links, half_block, axis=3), ahead, behind)
    solution = jnp.roll(moved, -half_block, axis=2)
    residual = source - full_operator(solution, links)
    return solution, residual
```

```python
import functools

import jax
import jax.numpy as jnp
from jax import lax
from jax.experimental import pallas as pl
from jax.experimental.pallas import tpu as pltpu
from jax.sharding import PartitionSpec as P


NMR = 4
DIAGONAL = 4.0 + 0.2
EPSILON = 1e-06
ENTRIES = 12 * 8 * 8 * 8
X, Y, Z, T = 0, 1, 2, 3
COLUMN = ((3, 2, 1, 0), (3, 2, 1, 0), (2, 3, 0, 1), (2, 3, 0, 1))
REAL = ((0, 0, 0, 0), (-1, 1, 1, -1), (0, 0, 0, 0), (1, 1, 1, 1))
IMAG = ((1, 1, -1, -1), (0, 0, 0, 0), (1, -1, -1, 1), (0, 0, 0, 0))
TILE = (8, 128)
F32 = jnp.float32


def lane_ids():
    return lax.broadcasted_iota(jnp.int32, TILE, 1)


def time_ids():
    return lax.broadcasted_iota(jnp.int32, TILE, 0)


def my_parity():
    return (lax.axis_index("gz") + lax.axis_index("ta")) % 2


def row_zero_first():
    return (lane_ids() // 8) % 2 == my_parity()


def lanes_by(value, steps):
    return pltpu.roll(value, steps % 128, 1)


def times_by(value, steps):
    return pltpu.roll(value, steps % 8, 0)


def add_gamma(base, orientation, direction, row, value):
    real = orientation * REAL[direction][row]
    imag = orientation * IMAG[direction][row]
    if real > 0:
        return (base[0] + value[0], base[1] + value[1])
    if real < 0:
        return (base[0] - value[0], base[1] - value[1])
    if imag > 0:
        return (base[0] - value[1], base[1] + value[0])
    return (base[0] + value[1], base[1] - value[0])


def project(field, direction, orientation):
    return [
        [
            add_gamma(
                field[row][color], orientation, direction, row, field[COLUMN[direction][row]][color]
            )
            for color in range(3)
        ]
        for row in range(2)
    ]


def expand_into(total, half, direction, orientation):
    for row in range(4):
        for color in range(3):
            if row < 2:
                base, value = total[row][color], half[row][color]
                total[row][color] = (base[0] + value[0], base[1] + value[1])
            else:
                total[row][color] = add_gamma(
                    total[row][color],
                    orientation,
                    direction,
                    row,
                    half[COLUMN[direction][row]][color],
                )


def color_apply(link, half, adjoint):
    result = []
    for row in range(2):
        out = []
        for a in range(3):
            real, imag = None, None
            for b in range(3):
                value = half[row][b]
                entry = link[b][a] if adjoint else link[a][b]
                if adjoint:
                    pr = entry[0] * value[0] + entry[1] * value[1]
                    pi = entry[0] * value[1] - entry[1] * value[0]
                else:
                    pr = entry[0] * value[0] - entry[1] * value[1]
                    pi = entry[0] * value[1] + entry[1] * value[0]
                real = pr if real is None else real + pr
                imag = pi if imag is None else imag + pi
            out.append((real, imag))
        result.append(out)
    return result


def map_half(function, half):
    return [[(function(v[0]), function(v[1])) for v in row] for row in half]


def load_link(get):
    return [[(get(a * 3 + b), get(9 + a * 3 + b)) for b in range(3)] for a in range(3)]


def load_spinor(ref):
    return [[(ref[s * 3 + c], ref[12 + s * 3 + c]) for c in range(3)] for s in range(4)]


def store_spinor(ref, field):
    for s in range(4):
        for c in range(3):
            ref[s * 3 + c] = field[s][c][0]
            ref[12 + s * 3 + c] = field[s][c][1]


def flat_half(half):
    return [half[s][c][part] for part in range(2) for s in range(2) for c in range(3)]


def unflat_half(flat):
    return [[(flat[s * 3 + c], flat[6 + s * 3 + c]) for c in range(3)] for s in range(2)]


def scaled(field, factor):
    return [[(factor * v[0], factor * v[1]) for v in row] for row in field]


def compact(ref, index, color, first):
    low = ref[index, :, 0:128]
    high = ref[index, :, 128:256]
    return jnp.where(first, low, high) if color == 0 else jnp.where(first, high, low)


def solve(rho_ref, w_ref, applied_ref, masked_ref, link):
    lane, time = lane_ids(), time_ids()
    inner = {X: lane % 8 != 7, Y: lane < 112, T: time != 7}
    for slot, direction in enumerate((X, Y, T)):
        for i in range(18):
            masked_ref[slot * 18 + i] = jnp.where(
                inner[direction], -0.5 * link(direction, i), 0.0
            )
    ahead = {
        X: lambda v: lanes_by(v, -1),
        Y: lambda v: lanes_by(v, -16),
        T: lambda v: times_by(v, -1),
    }
    behind = {
        X: lambda v: lanes_by(v, 1),
        Y: lambda v: lanes_by(v, 16),
        T: lambda v: times_by(v, 1),
    }
    left = (lane // 8) % 2 == 0

    def per_block(value):
        total_left = jnp.sum(jnp.where(left, value, 0.0), axis=(0, 1), keepdims=True)
        total_right = jnp.sum(jnp.where(left, 0.0, value), axis=(0, 1), keepdims=True)
        return jnp.where(left, total_left, total_right) / ENTRIES

    def step(_, carry):
        rho = load_spinor(rho_ref)
        total = scaled(rho, DIAGONAL)
        for slot, direction in enumerate((X, Y, T)):
            matrix = load_link(lambda i: masked_ref[slot * 18 + i])
            half = map_half(ahead[direction], project(rho, direction, -1))
            expand_into(total, color_apply(matrix, half, False), direction, -1)
            half = color_apply(matrix, project(rho, direction, 1), True)
            expand_into(total, map_half(behind[direction], half), direction, 1)
        store_spinor(applied_ref, total)
        real, imag, square = None, None, None
        for s in range(4):
            for c in range(3):
                (ar, ai), (rr, ri) = total[s][c], rho[s][c]
                pr = ar * rr + ai * ri
                pi = ar * ri - ai * rr
                ps = ar * ar + ai * ai
                real = pr if real is None else real + pr
                imag = pi if imag is None else imag + pi
                square = ps if square is None else square + ps
        denominator = per_block(square) + EPSILON
        weight_real = per_block(real) / denominator
        weight_imag = per_block(imag) / denominator
        for i in range(12):
            rr, ri = rho_ref[i], rho_ref[12 + i]
            ar, ai = applied_ref[i], applied_ref[12 + i]
            w_ref[i] = w_ref[i] + (weight_real * rr - weight_imag * ri)
            w_ref[12 + i] = w_ref[12 + i] + (weight_real * ri + weight_imag * rr)
            rho_ref[i] = rr - (weight_real * ar - weight_imag * ai)
            rho_ref[12 + i] = ri - (weight_real * ai + weight_imag * ar)
        return carry

    for i in range(24):
        w_ref[i] = jnp.zeros(TILE, F32)
    lax.fori_loop(0, NMR, step, 0)


def add_local_hops(total, half_w, link_to, link_from):
    lane = lane_ids()
    column = lane % 16

    def x_ahead(v):
        near = jnp.where(column == 7, lanes_by(v, -1), 0.0)
        return jnp.where(column == 15, lanes_by(v, 15), near)

    def x_behind(v):
        near = jnp.where(column == 8, lanes_by(v, 1), 0.0)
        return jnp.where(column == 0, lanes_by(v, -15), near)

    def y_ahead(v):
        return jnp.where(lane >= 112, lanes_by(v, -16), 0.0)

    def y_behind(v):
        return jnp.where(lane < 16, lanes_by(v, 16), 0.0)

    for direction, ahead, behind in ((X, x_ahead, x_behind), (Y, y_ahead, y_behind)):
        half = map_half(ahead, project(half_w, direction, -1))
        matrix = load_link(lambda i: link_to(direction, i))
        expand_into(total, color_apply(matrix, half, False), direction, -1)
        matrix = load_link(lambda i: link_from(direction, i))
        half = map_half(behind, color_apply(matrix, project(half_w, direction, 1), True))
        expand_into(total, half, direction, 1)


def outgoing(half_w, link_from, direction):
    matrix = load_link(lambda i: link_from(direction, i))
    ahead = color_apply(matrix, project(half_w, direction, 1), True)
    behind = project(half_w, direction, -1)
    return flat_half(ahead), flat_half(behind)


def store_rows(ref, flat, time):
    for i in range(12):
        ref[i : i + 1, :] = flat[i][time : time + 1, :]


def row_at(ref, time):
    here = time_ids() == time
    return unflat_half(
        [jnp.where(here, jnp.broadcast_to(ref[i : i + 1, :], TILE), 0.0) for i in range(12)]
    )


def store_faces(half_w, link_from, t_ahead_ref, t_behind_ref, z_ahead_ref, z_behind_ref):
    ahead, behind = outgoing(half_w, link_from, Z)
    for i in range(12):
        z_ahead_ref[i] = ahead[i]
        z_behind_ref[i] = behind[i]
    ahead, behind = outgoing(half_w, link_from, T)
    store_rows(t_ahead_ref, ahead, 7)
    store_rows(t_behind_ref, behind, 0)


def add_faces(total, link_to, t_low_ref, t_high_ref, z_low_ref, z_high_ref):
    expand_into(total, unflat_half([z_low_ref[i] for i in range(12)]), Z, 1)
    half = unflat_half([z_high_ref[i] for i in range(12)])
    matrix = load_link(lambda i: link_to(Z, i))
    expand_into(total, color_apply(matrix, half, False), Z, -1)
    expand_into(total, row_at(t_low_ref, 0), T, 1)
    matrix = load_link(lambda i: link_to(T, i))
    expand_into(total, color_apply(matrix, row_at(t_high_ref, 7), False), T, -1)


def store_split(half_w, link_from, lower, ahead_refs, behind_refs):
    low = time_ids() < 4
    for flat, (stay_ref, move_ref) in zip(
        outgoing(half_w, link_from, Z), (ahead_refs, behind_refs)
    ):
        for i in range(6):
            turned = times_by(flat[i], 4)
            straight = flat[i + 6]
            stay_ref[i] = jnp.where(low, straight, turned) if lower else jnp.where(low, turned, straight)
            move_ref[i] = jnp.where(low, turned, straight) if lower else jnp.where(low, straight, turned)


def join_split(low_ref, high_ref):
    low = time_ids() < 4
    flat = [jnp.where(low, low_ref[i], high_ref[i]) for i in range(6)]
    flat += [times_by(jnp.where(low, high_ref[i], low_ref[i]), 4) for i in range(6)]
    return unflat_half(flat)


def zero_spinor():
    zero = jnp.zeros(TILE, F32)
    return [[(zero, zero) for _ in range(3)] for _ in range(4)]


def split_faces(link_to, ahead_low, ahead_high, behind_low, behind_high):
    total = zero_spinor()
    expand_into(total, join_split(ahead_low, ahead_high), Z, 1)
    matrix = load_link(lambda i: link_to(Z, i))
    expand_into(total, color_apply(matrix, join_split(behind_low, behind_high), False), Z, -1)
    return total


def masked_spinor(field, mask):
    return [[(jnp.where(mask, v[0], 0.0), jnp.where(mask, v[1], 0.0)) for v in row] for row in field]


def add_spinor(total, other):
    for s in range(4):
        for c in range(3):
            a, b = total[s][c], other[s][c]
            total[s][c] = (a[0] + b[0], a[1] + b[1])


def raw_links(links_ref):
    first = row_zero_first()
    return [
        lambda direction, i, color=color: compact(links_ref, direction * 18 + i, color, first)
        for color in range(2)
    ]


def fill_moved_links(moved_ref, links_ref, received_ref):
    first = row_zero_first()
    low = time_ids() < 4
    for i in range(72):
        zero = times_by(compact(links_ref, i, 0, first), 4)
        one = times_by(compact(links_ref, i, 1, first), 4)
        other = received_ref[i]
        moved_ref[i] = jnp.where(low, other, zero)
        moved_ref[72 + i] = jnp.where(low, times_by(other, 4), one)


def moved_links(moved_ref):
    return [
        lambda direction, i, color=color: moved_ref[72 * color + direction * 18 + i]
        for color in range(2)
    ]


def pack_links_kernel(links_ref, out_ref):
    first = row_zero_first()
    low = time_ids() < 4
    for i in range(72):
        zero = compact(links_ref, i, 0, first)
        one = compact(links_ref, i, 1, first)
        out_ref[i] = jnp.where(low, times_by(one, 4), zero)


def kernel_one(links_ref, source_ref, w_ref, rho_ref, other_ref, ta_ref, tb_ref, za_ref, zb_ref,
               applied_ref, masked_ref):
    first = row_zero_first()
    link = raw_links(links_ref)
    for i in range(24):
        rho_ref[i] = compact(source_ref, i, 0, first)
        other_ref[i] = compact(source_ref, i, 1, first)
    solve(rho_ref, w_ref, applied_ref, masked_ref, link[0])
    half_w = scaled(load_spinor(w_ref), 0.5)
    store_faces(half_w, link[0], ta_ref, tb_ref, za_ref, zb_ref)
    total = load_spinor(other_ref)
    add_local_hops(total, half_w, link[1], link[0])
    store_spinor(other_ref, total)


def kernel_two(links_ref, rho_in, other_in, t_low, t_high, z_low, z_high,
               w_ref, rest_ref, rho_ref, send_ref, tb_ref, za_stay, za_move, zb_stay, zb_move,
               applied_ref, masked_ref):
    link = raw_links(links_ref)
    total = load_spinor(other_in)
    add_faces(total, link[1], t_low, t_high, z_low, z_high)
    store_spinor(rho_ref, total)
    solve(rho_ref, w_ref, applied_ref, masked_ref, link[1])
    half_w = scaled(load_spinor(w_ref), 0.5)
    store_split(half_w, link[1], True, (za_stay, za_move), (zb_stay, zb_move))
    ahead, behind = outgoing(half_w, link[1], T)
    store_rows(tb_ref, behind, 0)
    total = load_spinor(rho_in)
    add_local_hops(total, half_w, link[0], link[1])
    store_spinor(rest_ref, total)
    low = time_ids() < 4
    for i in range(24):
        send_ref[i] = jnp.where(low, times_by(rho_ref[i], 4), rest_ref[i])
    for i in range(12):
        send_ref[24 + i // 8, i % 8 : i % 8 + 1, :] = ahead[i][7:8, :]


class RowsOf:
    def __init__(self, ref, base):
        self.ref, self.base = ref, base

    def __getitem__(self, index):
        row = index[0].start
        return self.ref[self.base + row // 8, row % 8 : row % 8 + 1, :]


def kernel_three(links_ref, moved_in, rest_in, rho_in, received, tb_in, za_stay, za_move, zb_stay, zb_move,
                 w_ref, rho_ref, other_ref, ta_ref, tb_ref, za_ref, zb_ref,
                 applied_ref, masked_ref, moved_ref):
    fill_moved_links(moved_ref, links_ref, moved_in)
    link = moved_links(moved_ref)
    low = time_ids() < 4
    faces = split_faces(
        lambda direction, i: jnp.where(low, link[1](direction, i), link[0](direction, i)),
        za_move, za_stay, zb_move, zb_stay,
    )
    for i in range(24):
        other = received[i]
        rho_ref[i] = jnp.where(low, other, times_by(rest_in[i], 4))
        other_ref[i] = jnp.where(low, times_by(other, 4), times_by(rho_in[i], 4))
    total = load_spinor(rho_ref)
    add_spinor(total, masked_spinor(faces, jnp.logical_not(low)))
    expand_into(total, row_at(RowsOf(received, 24), 4), T, 1)
    store_spinor(rho_ref, total)
    total = load_spinor(other_ref)
    add_spinor(total, masked_spinor(faces, low))
    matrix = load_link(lambda i: link[1](T, i))
    expand_into(total, color_apply(matrix, row_at(tb_in, 3), False), T, -1)
    store_spinor(other_ref, total)
    solve(rho_ref, w_ref, applied_ref, masked_ref, link[0])
    half_w = scaled(load_spinor(w_ref), 0.5)
    store_faces(half_w, link[0], ta_ref, tb_ref, za_ref, zb_ref)
    total = load_spinor(other_ref)
    add_local_hops(total, half_w, link[1], link[0])
    store_spinor(other_ref, total)


def kernel_four(links_ref, moved_in, w_in, rho_in, other_in, t_low, t_high, z_low, z_high,
                w_ref, rest_ref, rho_ref, send_ref, ta_ref, za_stay, za_move, zb_stay, zb_move,
                applied_ref, masked_ref, moved_ref):
    fill_moved_links(moved_ref, links_ref, moved_in)
    link = moved_links(moved_ref)
    total = load_spinor(other_in)
    add_faces(total, link[1], t_low, t_high, z_low, z_high)
    store_spinor(rho_ref, total)
    solve(rho_ref, w_ref, applied_ref, masked_ref, link[1])
    half_w = scaled(load_spinor(w_ref), 0.5)
    store_split(half_w, link[1], False, (za_stay, za_move), (zb_stay, zb_move))
    ahead, behind = outgoing(half_w, link[1], T)
    store_rows(ta_ref, ahead, 7)
    total = load_spinor(rho_in)
    add_local_hops(total, half_w, link[0], link[1])
    store_spinor(rest_ref, total)
    low = time_ids() < 4
    for i in range(24):
        send_ref[i] = jnp.where(low, rho_ref[i], times_by(rest_ref[i], 4))
        send_ref[24 + i] = jnp.where(low, w_ref[i], times_by(w_in[i], 4))
    for i in range(12):
        send_ref[48 + i // 8, i % 8 : i % 8 + 1, :] = behind[i][0:1, :]


def kernel_five(links_ref, w0_ref, w1_ref, x0_ref, x1_ref, rest_in, rho_in, received, ta_in,
                za_stay, za_move, zb_stay, zb_move, solution_ref, residual_ref):
    link = raw_links(links_ref)
    first = row_zero_first()
    low = time_ids() < 4

    def put(ref, i, zero, one):
        ref[i, :, 0:128] = jnp.where(first, zero, one)
        ref[i, :, 128:256] = jnp.where(first, one, zero)

    for i in range(24):
        other = received[24 + i]
        zero = jnp.where(low, times_by(x0_ref[i], 4), times_by(other, 4))
        one = jnp.where(low, times_by(x1_ref[i], 4), other)
        put(solution_ref, i, w0_ref[i] + zero, w1_ref[i] + one)
    faces = split_faces(
        lambda direction, i: jnp.where(low, link[0](direction, i), link[1](direction, i)),
        za_stay, za_move, zb_stay, zb_move,
    )
    zero, one = masked_spinor(faces, low), masked_spinor(faces, jnp.logical_not(low))
    matrix = load_link(lambda i: link[0](T, i))
    expand_into(zero, color_apply(matrix, row_at(RowsOf(received, 48), 3), False), T, -1)
    expand_into(one, row_at(ta_in, 4), T, 1)
    for s in range(4):
        for c in range(3):
            for part in range(2):
                i = part * 12 + s * 3 + c
                other = received[i]
                base_zero = jnp.where(low, times_by(rest_in[i], 4), times_by(other, 4))
                base_one = jnp.where(low, times_by(rho_in[i], 4), other)
                put(residual_ref, i, base_zero + zero[s][c][part], base_one + one[s][c][part])


def call(kernel, shapes, operands, solver=False, moved=False, cost=3000000):
    scratch = []
    if solver:
        scratch = [pltpu.VMEM((24,) + TILE, F32), pltpu.VMEM((54,) + TILE, F32)]
    if moved:
        scratch.append(pltpu.VMEM((144,) + TILE, F32))
    vmem = pl.BlockSpec(memory_space=pltpu.VMEM)
    return pl.pallas_call(
        kernel,
        out_shape=[jax.ShapeDtypeStruct(shape, F32) for shape in shapes],
        in_specs=[vmem] * len(operands),
        out_specs=[vmem] * len(shapes),
        scratch_shapes=scratch,
        cost_estimate=pl.CostEstimate(flops=cost, bytes_accessed=cost // 2, transcendentals=0),
    )(*operands)


def moved_to(value, time_steps, depth_steps):
    times, depths = lax.axis_size("ta"), lax.axis_size("gz")
    if depth_steps == 0:
        return lax.ppermute(value, "ta", [(i, (i + time_steps) % times) for i in range(times)])
    if time_steps == 0:
        return lax.ppermute(value, "gz", [(i, (i + depth_steps) % depths) for i in range(depths)])
    pairs = [
        (t * depths + g, (t + time_steps) % times * depths + (g + depth_steps) % depths)
        for t in range(times)
        for g in range(depths)
    ]
    return lax.ppermute(value, ("ta", "gz"), pairs)


def per_device(links, source):
    links = links.reshape((72, 8, 256))
    source = source.reshape((24, 8, 256))
    spinor, half, quarter, rows = (24,) + TILE, (12,) + TILE, (6,) + TILE, (12, 128)
    (packed,) = call(pack_links_kernel, [(72,) + TILE], [links])
    moved = moved_to(packed, 1, 0)

    w0, rho0, other, ta, tb, za, zb = call(
        kernel_one, [spinor] * 3 + [rows] * 2 + [half] * 2, [links, source], solver=True
    )
    faces = [moved_to(ta, 1, 0), moved_to(tb, -1, 0), moved_to(za, 0, 1), moved_to(zb, 0, -1)]
    w1, rest, rho1, send, tb, za_stay, za_move, zb_stay, zb_move = call(
        kernel_two,
        [spinor] * 3 + [(26,) + TILE, rows] + [quarter] * 4,
        [links, rho0, other] + faces,
        solver=True,
    )
    received = [
        moved_to(send, 1, 0),
        tb,
        moved_to(za_stay, 0, 1),
        moved_to(za_move, 1, 1),
        moved_to(zb_stay, 0, -1),
        moved_to(zb_move, 1, -1),
    ]
    x0, rho0, other, ta, tb, za, zb = call(
        kernel_three,
        [spinor] * 3 + [rows] * 2 + [half] * 2,
        [links, moved, rest, rho1] + received,
        solver=True,
        moved=True,
    )
    faces = [moved_to(ta, 1, 0), moved_to(tb, -1, 0), moved_to(za, 0, 1), moved_to(zb, 0, -1)]
    x1, rest, rho1, send, ta, za_stay, za_move, zb_stay, zb_move = call(
        kernel_four,
        [spinor] * 3 + [(50,) + TILE, rows] + [quarter] * 4,
        [links, moved, x0, rho0, other] + faces,
        solver=True,
        moved=True,
    )
    received = [
        moved_to(send, -1, 0),
        ta,
        moved_to(za_stay, 0, 1),
        moved_to(za_move, -1, 1),
        moved_to(zb_stay, 0, -1),
        moved_to(zb_move, -1, -1),
    ]
    solution, residual = call(
        kernel_five, [(24, 8, 256)] * 2, [links, w0, w1, x0, x1, rest, rho1] + received
    )
    return solution.reshape((24, 1, 8, 256)), residual.reshape((24, 1, 8, 256))


def solution(mesh):
    in_specs = (P(None, None, "gz", "ta", None), P(None, "gz", "ta", None))
    out_specs = (P(None, "gz", "ta", None), P(None, "gz", "ta", None))
    return jax.shard_map(
        per_device, mesh=mesh, in_specs=in_specs, out_specs=out_specs, check_vma=False
    )
```

```python
import jax
import jax.numpy as jnp
from jax import lax
from jax.experimental import pallas as pl
from jax.experimental.pallas import tpu as pltpu
from jax.sharding import PartitionSpec as P


NMR = 4
DIAGONAL = 4.0 + 0.2
EPSILON = 1e-06
ENTRIES = 12 * 8 * 8 * 8
X, Y, Z, T = 0, 1, 2, 3
COLUMN = ((3, 2, 1, 0), (3, 2, 1, 0), (2, 3, 0, 1), (2, 3, 0, 1))
REAL = ((0, 0, 0, 0), (-1, 1, 1, -1), (0, 0, 0, 0), (1, 1, 1, 1))
IMAG = ((1, 1, -1, -1), (0, 0, 0, 0), (1, -1, -1, 1), (0, 0, 0, 0))
TILE = (8, 128)
F32 = jnp.float32


def lane_ids():
    return lax.broadcasted_iota(jnp.int32, TILE, 1)


def time_ids():
    return lax.broadcasted_iota(jnp.int32, TILE, 0)


def my_parity():
    return (lax.axis_index("gz") + lax.axis_index("ta")) % 2


def row_zero_first():
    return (lane_ids() // 8) % 2 == my_parity()


def is_even(axis):
    return (lane_ids() * 0 + lax.axis_index(axis)) % 2 == 0


def lanes_by(value, steps):
    return pltpu.roll(value, steps % 128, 1)


def times_by(value, steps):
    return pltpu.roll(value, steps % 8, 0)


def add_gamma(base, orientation, direction, row, value):
    real = orientation * REAL[direction][row]
    imag = orientation * IMAG[direction][row]
    if real > 0:
        return (base[0] + value[0], base[1] + value[1])
    if real < 0:
        return (base[0] - value[0], base[1] - value[1])
    if imag > 0:
        return (base[0] - value[1], base[1] + value[0])
    return (base[0] + value[1], base[1] - value[0])


def project(field, direction, orientation):
    return [
        [
            add_gamma(
                field[row][color], orientation, direction, row, field[COLUMN[direction][row]][color]
            )
            for color in range(3)
        ]
        for row in range(2)
    ]


def expand_into(total, half, direction, orientation):
    for row in range(4):
        for color in range(3):
            if row < 2:
                base, value = total[row][color], half[row][color]
                total[row][color] = (base[0] + value[0], base[1] + value[1])
            else:
                total[row][color] = add_gamma(
                    total[row][color],
                    orientation,
                    direction,
                    row,
                    half[COLUMN[direction][row]][color],
                )


def color_apply(link, half, adjoint):
    result = []
    for row in range(2):
        out = []
        for a in range(3):
            real, imag = None, None
            for b in range(3):
                value = half[row][b]
                entry = link[b][a] if adjoint else link[a][b]
                if adjoint:
                    pr = entry[0] * value[0] + entry[1] * value[1]
                    pi = entry[0] * value[1] - entry[1] * value[0]
                else:
                    pr = entry[0] * value[0] - entry[1] * value[1]
                    pi = entry[0] * value[1] + entry[1] * value[0]
                real = pr if real is None else real + pr
                imag = pi if imag is None else imag + pi
            out.append((real, imag))
        result.append(out)
    return result


def map_half(function, half):
    return [[(function(v[0]), function(v[1])) for v in row] for row in half]


def load_link(get):
    return [[(get(a * 3 + b), get(9 + a * 3 + b)) for b in range(3)] for a in range(3)]


def load_spinor(ref):
    return [[(ref[s * 3 + c], ref[12 + s * 3 + c]) for c in range(3)] for s in range(4)]


def store_spinor(ref, field):
    for s in range(4):
        for c in range(3):
            ref[s * 3 + c] = field[s][c][0]
            ref[12 + s * 3 + c] = field[s][c][1]


def flat_half(half):
    return [half[s][c][part] for part in range(2) for s in range(2) for c in range(3)]


def unflat_half(flat):
    return [[(flat[s * 3 + c], flat[6 + s * 3 + c]) for c in range(3)] for s in range(2)]


def scaled(field, factor):
    return [[(factor * v[0], factor * v[1]) for v in row] for row in field]


def compact(ref, index, color, first):
    low = ref[index, :, 0:128]
    high = ref[index, :, 128:256]
    return jnp.where(first, low, high) if color == 0 else jnp.where(first, high, low)


def solve(rho_ref, w_ref, applied_ref, masked_ref, link):
    lane, time = lane_ids(), time_ids()
    inner = {X: lane % 8 != 7, Y: lane < 112, T: time != 7}
    for slot, direction in enumerate((X, Y, T)):
        for i in range(18):
            masked_ref[slot * 18 + i] = jnp.where(
                inner[direction], -0.5 * link(direction, i), 0.0
            )
    ahead = {
        X: lambda v: lanes_by(v, -1),
        Y: lambda v: lanes_by(v, -16),
        T: lambda v: times_by(v, -1),
    }
    behind = {
        X: lambda v: lanes_by(v, 1),
        Y: lambda v: lanes_by(v, 16),
        T: lambda v: times_by(v, 1),
    }
    left = (lane // 8) % 2 == 0

    def per_block(value):
        total_left = jnp.sum(jnp.where(left, value, 0.0), axis=(0, 1), keepdims=True)
        total_right = jnp.sum(jnp.where(left, 0.0, value), axis=(0, 1), keepdims=True)
        return jnp.where(left, total_left, total_right) / ENTRIES

    def step(_, carry):
        rho = load_spinor(rho_ref)
        total = scaled(rho, DIAGONAL)
        for slot, direction in enumerate((X, Y, T)):
            matrix = load_link(lambda i: masked_ref[slot * 18 + i])
            half = map_half(ahead[direction], project(rho, direction, -1))
            expand_into(total, color_apply(matrix, half, False), direction, -1)
            half = color_apply(matrix, project(rho, direction, 1), True)
            expand_into(total, map_half(behind[direction], half), direction, 1)
        store_spinor(applied_ref, total)
        real, imag, square = None, None, None
        for s in range(4):
            for c in range(3):
                (ar, ai), (rr, ri) = total[s][c], rho[s][c]
                pr = ar * rr + ai * ri
                pi = ar * ri - ai * rr
                ps = ar * ar + ai * ai
                real = pr if real is None else real + pr
                imag = pi if imag is None else imag + pi
                square = ps if square is None else square + ps
        denominator = per_block(square) + EPSILON
        weight_real = per_block(real) / denominator
        weight_imag = per_block(imag) / denominator
        for i in range(12):
            rr, ri = rho_ref[i], rho_ref[12 + i]
            ar, ai = applied_ref[i], applied_ref[12 + i]
            w_ref[i] = w_ref[i] + (weight_real * rr - weight_imag * ri)
            w_ref[12 + i] = w_ref[12 + i] + (weight_real * ri + weight_imag * rr)
            rho_ref[i] = rr - (weight_real * ar - weight_imag * ai)
            rho_ref[12 + i] = ri - (weight_real * ai + weight_imag * ar)
        return carry

    for i in range(24):
        w_ref[i] = jnp.zeros(TILE, F32)
    lax.fori_loop(0, NMR, step, 0)


def add_local_hops(total, half_w, link_to, link_from):
    lane = lane_ids()
    column = lane % 16

    def x_ahead(v):
        near = jnp.where(column == 7, lanes_by(v, -1), 0.0)
        return jnp.where(column == 15, lanes_by(v, 15), near)

    def x_behind(v):
        near = jnp.where(column == 8, lanes_by(v, 1), 0.0)
        return jnp.where(column == 0, lanes_by(v, -15), near)

    def y_ahead(v):
        return jnp.where(lane >= 112, lanes_by(v, -16), 0.0)

    def y_behind(v):
        return jnp.where(lane < 16, lanes_by(v, 16), 0.0)

    for direction, ahead, behind in ((X, x_ahead, x_behind), (Y, y_ahead, y_behind)):
        half = map_half(ahead, project(half_w, direction, -1))
        matrix = load_link(lambda i: link_to(direction, i))
        expand_into(total, color_apply(matrix, half, False), direction, -1)
        matrix = load_link(lambda i: link_from(direction, i))
        half = map_half(behind, color_apply(matrix, project(half_w, direction, 1), True))
        expand_into(total, half, direction, 1)


def outgoing(half_w, link_from, direction):
    matrix = load_link(lambda i: link_from(direction, i))
    ahead = color_apply(matrix, project(half_w, direction, 1), True)
    behind = project(half_w, direction, -1)
    return flat_half(ahead), flat_half(behind)


def store_pairs(even, ahead, behind, first_ref, second_ref):
    for i in range(len(ahead)):
        first_ref[i] = jnp.where(even, ahead[i], behind[i])
        second_ref[i] = jnp.where(even, behind[i], ahead[i])


def load_pairs(even, first, second):
    low = [jnp.where(even, b, a) for a, b in zip(first, second)]
    high = [jnp.where(even, a, b) for a, b in zip(first, second)]
    return low, high


def store_rows(ref, index, row):
    ref[index : index + 1, :] = row


def row_at(ref, time):
    here = time_ids() == time
    return unflat_half(
        [jnp.where(here, jnp.broadcast_to(ref[i : i + 1, :], TILE), 0.0) for i in range(12)]
    )


def store_faces(half_w, depth_half_w, link_from, t_refs, z_refs):
    ahead, behind = outgoing(depth_half_w, link_from, Z)
    store_pairs(is_even("gz"), ahead, behind, *z_refs)
    ahead, behind = outgoing(half_w, link_from, T)
    even = is_even("ta")[0:1, :]
    for i in range(12):
        low, high = behind[i][0:1, :], ahead[i][7:8, :]
        store_rows(t_refs[0], i, jnp.where(even, high, low))
        store_rows(t_refs[1], i, jnp.where(even, low, high))


def add_faces(total, link_to, t_refs, z_refs):
    low, high = load_pairs(
        is_even("gz"), [z_refs[0][i] for i in range(12)], [z_refs[1][i] for i in range(12)]
    )
    expand_into(total, unflat_half(low), Z, 1)
    matrix = load_link(lambda i: link_to(Z, i))
    expand_into(total, color_apply(matrix, unflat_half(high), False), Z, -1)
    time = time_ids()
    rows = [
        [jnp.broadcast_to(ref[i : i + 1, :], TILE) for i in range(12)] for ref in t_refs
    ]
    low, high = load_pairs(is_even("ta"), *rows)
    low = unflat_half([jnp.where(time == 0, v, 0.0) for v in low])
    high = unflat_half([jnp.where(time == 7, v, 0.0) for v in high])
    expand_into(total, low, T, 1)
    matrix = load_link(lambda i: link_to(T, i))
    expand_into(total, color_apply(matrix, high, False), T, -1)


def packed_lower(flat):
    low = time_ids() < 4
    return [jnp.where(low, flat[i + 6], times_by(flat[i], 4)) for i in range(6)]


def unpacked_lower(tiles):
    low = time_ids() < 4
    flat = [jnp.where(low, 0.0, v) for v in tiles]
    flat += [jnp.where(low, 0.0, times_by(v, 4)) for v in tiles]
    return unflat_half(flat)


def packed_split(flat):
    low = time_ids() < 4
    stay, move = [], []
    for i in range(6):
        turned = times_by(flat[i], 4)
        stay.append(jnp.where(low, turned, flat[i + 6]))
        move.append(jnp.where(low, flat[i + 6], turned))
    return stay, move


def join_split(low_tiles, high_tiles):
    low = time_ids() < 4
    flat = [jnp.where(low, a, b) for a, b in zip(low_tiles, high_tiles)]
    flat += [times_by(jnp.where(low, b, a), 4) for a, b in zip(low_tiles, high_tiles)]
    return unflat_half(flat)


def zero_spinor():
    zero = jnp.zeros(TILE, F32)
    return [[(zero, zero) for _ in range(3)] for _ in range(4)]


def masked_spinor(field, mask):
    return [[(jnp.where(mask, v[0], 0.0), jnp.where(mask, v[1], 0.0)) for v in row] for row in field]


def add_spinor(total, other):
    for s in range(4):
        for c in range(3):
            a, b = total[s][c], other[s][c]
            total[s][c] = (a[0] + b[0], a[1] + b[1])


def raw_links(links_ref):
    first = row_zero_first()
    return [
        lambda direction, i, color=color: compact(links_ref, direction * 18 + i, color, first)
        for color in range(2)
    ]


def fill_moved_links(moved_ref, links_ref, received_ref):
    first = row_zero_first()
    low = time_ids() < 4
    for i in range(72):
        zero = times_by(compact(links_ref, i, 0, first), 4)
        one = times_by(compact(links_ref, i, 1, first), 4)
        other = received_ref[i]
        moved_ref[i] = jnp.where(low, other, zero)
        moved_ref[72 + i] = jnp.where(low, times_by(other, 4), one)


def moved_links(moved_ref):
    return [
        lambda direction, i, color=color: moved_ref[72 * color + direction * 18 + i]
        for color in range(2)
    ]


def pack_links_kernel(links_ref, out_ref):
    first = row_zero_first()
    low = time_ids() < 4
    for i in range(72):
        zero = compact(links_ref, i, 0, first)
        one = compact(links_ref, i, 1, first)
        out_ref[i] = jnp.where(low, times_by(one, 4), zero)


def kernel_one(links_ref, source_ref, w_ref, rho_ref, other_ref, t0_ref, t1_ref, z0_ref, z1_ref,
               applied_ref, masked_ref):
    first = row_zero_first()
    link = raw_links(links_ref)
    for i in range(24):
        rho_ref[i] = compact(source_ref, i, 0, first)
        other_ref[i] = compact(source_ref, i, 1, first)
    solve(rho_ref, w_ref, applied_ref, masked_ref, link[0])
    half_w = scaled(load_spinor(w_ref), 0.5)
    store_faces(half_w, half_w, link[0], (t0_ref, t1_ref), (z0_ref, z1_ref))
    total = load_spinor(other_ref)
    add_local_hops(total, half_w, link[1], link[0])
    store_spinor(other_ref, total)


def kernel_two(links_ref, rho_in, other_in, t0_in, t1_in, z0_in, z1_in,
               w_ref, rest_ref, rho_ref, send_ref, tb_ref, z0_ref, z1_ref,
               applied_ref, masked_ref):
    link = raw_links(links_ref)
    total = load_spinor(other_in)
    add_faces(total, link[1], (t0_in, t1_in), (z0_in, z1_in))
    store_spinor(rho_ref, total)
    solve(rho_ref, w_ref, applied_ref, masked_ref, link[1])
    half_w = scaled(load_spinor(w_ref), 0.5)
    ahead, behind = outgoing(half_w, link[1], Z)
    store_pairs(is_even("gz"), packed_lower(ahead), packed_lower(behind), z0_ref, z1_ref)
    behind = flat_half(project(half_w, T, -1))
    for i in range(12):
        store_rows(tb_ref, i, behind[i][0:1, :])
    total = load_spinor(rho_in)
    add_local_hops(total, half_w, link[0], link[1])
    store_spinor(rest_ref, total)
    low = time_ids() < 4
    for i in range(24):
        send_ref[i] = jnp.where(low, times_by(rho_ref[i], 4), rest_ref[i])
    for i in range(12):
        send_ref[24 + i] = jnp.where(low, times_by(w_ref[i], 4), w_ref[12 + i])


def kernel_three(links_ref, moved_in, rest_in, rho_in, tb_in, received, z0_in, z1_in,
                 w_ref, rho_ref, other_ref, t0_ref, t1_ref, z0_ref, z1_ref,
                 applied_ref, masked_ref, moved_ref):
    fill_moved_links(moved_ref, links_ref, moved_in)
    link = moved_links(moved_ref)
    time = time_ids()
    low = time < 4
    for i in range(24):
        other = received[i]
        rho_ref[i] = jnp.where(low, other, times_by(rest_in[i], 4))
        other_ref[i] = jnp.where(low, times_by(other, 4), times_by(rho_in[i], 4))
    came = [jnp.where(low, 0.5 * received[24 + i], 0.0) for i in range(12)]
    came += [jnp.where(low, 0.5 * times_by(received[24 + i], 4), 0.0) for i in range(12)]
    came = [[(came[s * 3 + c], came[12 + s * 3 + c]) for c in range(3)] for s in range(4)]
    total = load_spinor(rho_ref)
    lower, higher = load_pairs(
        is_even("gz"), [z0_in[i] for i in range(6)], [z1_in[i] for i in range(6)]
    )
    expand_into(total, unpacked_lower(lower), Z, 1)
    matrix = load_link(lambda i: link[0](Z, i))
    expand_into(total, color_apply(matrix, unpacked_lower(higher), False), Z, -1)
    matrix = load_link(lambda i: link[0](T, i))
    half = color_apply(matrix, project(came, T, 1), True)
    half = map_half(lambda v: jnp.where(time == 4, times_by(v, 1), 0.0), half)
    expand_into(total, half, T, 1)
    store_spinor(rho_ref, total)
    total = load_spinor(other_ref)
    matrix = load_link(lambda i: link[1](T, i))
    expand_into(total, color_apply(matrix, row_at(tb_in, 3), False), T, -1)
    store_spinor(other_ref, total)
    solve(rho_ref, w_ref, applied_ref, masked_ref, link[0])
    half_w = scaled(load_spinor(w_ref), 0.5)
    depth_half_w = came
    add_spinor(depth_half_w, half_w)
    store_faces(half_w, depth_half_w, link[0], (t0_ref, t1_ref), (z0_ref, z1_ref))
    total = load_spinor(other_ref)
    add_local_hops(total, half_w, link[1], link[0])
    store_spinor(other_ref, total)


def kernel_four(links_ref, moved_in, w_in, rho_in, other_in, t0_in, t1_in, z0_in, z1_in,
                w_ref, rest_ref, rho_ref, send_ref, ta_ref, z0_ref, z1_ref, za_ref, zb_ref,
                applied_ref, masked_ref, moved_ref):
    fill_moved_links(moved_ref, links_ref, moved_in)
    link = moved_links(moved_ref)
    total = load_spinor(other_in)
    add_faces(total, link[1], (t0_in, t1_in), (z0_in, z1_in))
    store_spinor(rho_ref, total)
    solve(rho_ref, w_ref, applied_ref, masked_ref, link[1])
    half_w = scaled(load_spinor(w_ref), 0.5)
    ahead, behind = outgoing(half_w, link[1], Z)
    ahead, ahead_move = packed_split(ahead)
    behind, behind_move = packed_split(behind)
    store_pairs(is_even("gz"), ahead, behind, z0_ref, z1_ref)
    for i in range(6):
        za_ref[i] = ahead_move[i]
        zb_ref[i] = behind_move[i]
    matrix = load_link(lambda i: link[1](T, i))
    ahead = flat_half(color_apply(matrix, project(half_w, T, 1), True))
    for i in range(12):
        store_rows(ta_ref, i, ahead[i][7:8, :])
    total = load_spinor(rho_in)
    add_local_hops(total, half_w, link[0], link[1])
    store_spinor(rest_ref, total)
    low = time_ids() < 4
    for i in range(24):
        send_ref[i] = jnp.where(low, rho_ref[i], times_by(rest_ref[i], 4))
        send_ref[24 + i] = jnp.where(low, w_ref[i], times_by(w_in[i], 4))


def kernel_five(links_ref, w0_ref, w1_ref, x0_ref, x1_ref, rest_in, rho_in, ta_in, received,
                z0_in, z1_in, za_in, zb_in, solution_ref, residual_ref):
    link = raw_links(links_ref)
    first = row_zero_first()
    time = time_ids()
    low = time < 4

    def put(ref, i, zero, one):
        ref[i, :, 0:128] = jnp.where(first, zero, one)
        ref[i, :, 128:256] = jnp.where(first, one, zero)

    update = []
    for i in range(24):
        other = received[24 + i]
        zero = jnp.where(low, times_by(x0_ref[i], 4), times_by(other, 4))
        one = jnp.where(low, times_by(x1_ref[i], 4), other)
        put(solution_ref, i, w0_ref[i] + zero, w1_ref[i] + one)
        update.append(zero)
    lower, higher = load_pairs(
        is_even("gz"), [z0_in[i] for i in range(6)], [z1_in[i] for i in range(6)]
    )
    faces = zero_spinor()
    expand_into(faces, join_split(lower, [za_in[i] for i in range(6)]), Z, 1)
    matrix = load_link(lambda i: jnp.where(low, link[0](Z, i), link[1](Z, i)))
    half = join_split(higher, [zb_in[i] for i in range(6)])
    expand_into(faces, color_apply(matrix, half, False), Z, -1)
    zero, one = masked_spinor(faces, low), masked_spinor(faces, jnp.logical_not(low))
    update = [
        [(0.5 * update[s * 3 + c], 0.5 * update[12 + s * 3 + c]) for c in range(3)] for s in range(4)
    ]
    half = map_half(
        lambda v: jnp.where(time == 3, times_by(v, -1), 0.0), project(update, T, -1)
    )
    matrix = load_link(lambda i: link[0](T, i))
    expand_into(zero, color_apply(matrix, half, False), T, -1)
    expand_into(one, row_at(ta_in, 4), T, 1)
    for s in range(4):
        for c in range(3):
            for part in range(2):
                i = part * 12 + s * 3 + c
                other = received[i]
                base_zero = jnp.where(low, times_by(rest_in[i], 4), times_by(other, 4))
                base_one = jnp.where(low, times_by(rho_in[i], 4), other)
                put(residual_ref, i, base_zero + zero[s][c][part], base_one + one[s][c][part])


def call(kernel, shapes, operands, solver=False, moved=False, cost=3000000):
    scratch = []
    if solver:
        scratch = [pltpu.VMEM((24,) + TILE, F32), pltpu.VMEM((54,) + TILE, F32)]
    if moved:
        scratch.append(pltpu.VMEM((144,) + TILE, F32))
    vmem = pl.BlockSpec(memory_space=pltpu.VMEM)
    return pl.pallas_call(
        kernel,
        out_shape=[jax.ShapeDtypeStruct(shape, F32) for shape in shapes],
        in_specs=[vmem] * len(operands),
        out_specs=[vmem] * len(shapes),
        scratch_shapes=scratch,
        compiler_params=pltpu.CompilerParams(vmem_limit_bytes=12 << 20),
        cost_estimate=pl.CostEstimate(flops=cost, bytes_accessed=cost // 2, transcendentals=0),
    )(*operands)


def moved_to(value, time_steps, depth_steps):
    times, depths = lax.axis_size("ta"), lax.axis_size("gz")
    if depth_steps == 0:
        return lax.ppermute(value, "ta", [(i, (i + time_steps) % times) for i in range(times)])
    pairs = [
        (t * depths + g, (t + time_steps) % times * depths + (g + depth_steps) % depths)
        for t in range(times)
        for g in range(depths)
    ]
    return lax.ppermute(value, ("ta", "gz"), pairs)


def exchanged(value, axis, odd):
    count = lax.axis_size(axis)
    pairs = [(i, (i + (1 if i % 2 == odd else -1)) % count) for i in range(count)]
    return lax.ppermute(value, axis, pairs)


def exchange_faces(t0, t1, z0, z1):
    z0 = exchanged(z0, "gz", 0)
    t0 = exchanged(t0, "ta", 0)
    z1 = exchanged(z1, "gz", 1)
    t1 = exchanged(t1, "ta", 1)
    return [t0, t1, z0, z1]


def per_device(links, source):
    links = links.reshape((72, 8, 256))
    source = source.reshape((24, 8, 256))
    spinor, half, quarter, rows = (24,) + TILE, (12,) + TILE, (6,) + TILE, (12, 128)
    faces = [rows] * 2 + [half] * 2
    (packed,) = call(pack_links_kernel, [(72,) + TILE], [links])
    moved = moved_to(packed, 1, 0)

    w0, rho0, other, *sent = call(kernel_one, [spinor] * 3 + faces, [links, source], solver=True)
    came = exchange_faces(*sent)
    w1, rest, rho1, send, tb, z0, z1 = call(
        kernel_two,
        [spinor] * 3 + [(36,) + TILE, rows, quarter, quarter],
        [links, rho0, other] + came,
        solver=True,
    )
    z0 = exchanged(z0, "gz", 0)
    z1 = exchanged(z1, "gz", 1)
    send = moved_to(send, 1, 0)
    x0, rho0, other, *sent = call(
        kernel_three,
        [spinor] * 3 + faces,
        [links, moved, rest, rho1, tb, send, z0, z1],
        solver=True,
        moved=True,
    )
    came = exchange_faces(*sent)
    x1, rest, rho1, send, ta, z0, z1, za, zb = call(
        kernel_four,
        [spinor] * 3 + [(48,) + TILE, rows] + [quarter] * 4,
        [links, moved, x0, rho0, other] + came,
        solver=True,
        moved=True,
    )
    z0 = exchanged(z0, "gz", 0)
    z1 = exchanged(z1, "gz", 1)
    send = moved_to(send, -1, 0)
    za = moved_to(za, -1, 1)
    zb = moved_to(zb, -1, -1)
    solution, residual = call(
        kernel_five,
        [(24, 8, 256)] * 2,
        [links, w0, w1, x0, x1, rest, rho1, ta, send, z0, z1, za, zb],
    )
    return solution.reshape((24, 1, 8, 256)), residual.reshape((24, 1, 8, 256))


def solution(mesh):
    in_specs = (P(None, None, "gz", "ta", None), P(None, "gz", "ta", None))
    out_specs = (P(None, "gz", "ta", None), P(None, "gz", "ta", None))
    return jax.shard_map(
        per_device, mesh=mesh, in_specs=in_specs, out_specs=out_specs, check_vma=False
    )
```

```python
import jax
import jax.numpy as jnp
from jax import lax
from jax.experimental import pallas as pl
from jax.experimental.pallas import tpu as pltpu
from jax.sharding import PartitionSpec as P


NMR = 4
DIAGONAL = 4.0 + 0.2
EPSILON = 1e-06
ENTRIES = 12 * 8 * 8 * 8
X, Y, Z, T = 0, 1, 2, 3
COLUMN = ((3, 2, 1, 0), (3, 2, 1, 0), (2, 3, 0, 1), (2, 3, 0, 1))
REAL = ((0, 0, 0, 0), (-1, 1, 1, -1), (0, 0, 0, 0), (1, 1, 1, 1))
IMAG = ((1, 1, -1, -1), (0, 0, 0, 0), (1, -1, -1, 1), (0, 0, 0, 0))
TILE = (8, 128)
F32 = jnp.float32


def lane_ids():
    return lax.broadcasted_iota(jnp.int32, TILE, 1)


def time_ids():
    return lax.broadcasted_iota(jnp.int32, TILE, 0)


def my_parity():
    return (lax.axis_index("gz") + lax.axis_index("ta")) % 2


def row_zero_first():
    return (lane_ids() // 8) % 2 == my_parity()


def is_even(axis):
    return (lane_ids() * 0 + lax.axis_index(axis)) % 2 == 0


def lanes_by(value, steps):
    return pltpu.roll(value, steps % 128, 1)


def times_by(value, steps):
    return pltpu.roll(value, steps % 8, 0)


def add_gamma(base, orientation, direction, row, value):
    real = orientation * REAL[direction][row]
    imag = orientation * IMAG[direction][row]
    if real > 0:
        return (base[0] + value[0], base[1] + value[1])
    if real < 0:
        return (base[0] - value[0], base[1] - value[1])
    if imag > 0:
        return (base[0] - value[1], base[1] + value[0])
    return (base[0] + value[1], base[1] - value[0])


def project(field, direction, orientation):
    return [
        [
            add_gamma(
                field[row][color], orientation, direction, row, field[COLUMN[direction][row]][color]
            )
            for color in range(3)
        ]
        for row in range(2)
    ]


def expand_into(total, half, direction, orientation):
    for row in range(4):
        for color in range(3):
            if row < 2:
                base, value = total[row][color], half[row][color]
                total[row][color] = (base[0] + value[0], base[1] + value[1])
            else:
                total[row][color] = add_gamma(
                    total[row][color],
                    orientation,
                    direction,
                    row,
                    half[COLUMN[direction][row]][color],
                )


def color_apply(link, half, adjoint):
    result = []
    for row in range(2):
        out = []
        for a in range(3):
            real, imag = None, None
            for b in range(3):
                value = half[row][b]
                entry = link[b][a] if adjoint else link[a][b]
                if adjoint:
                    pr = entry[0] * value[0] + entry[1] * value[1]
                    pi = entry[0] * value[1] - entry[1] * value[0]
                else:
                    pr = entry[0] * value[0] - entry[1] * value[1]
                    pi = entry[0] * value[1] + entry[1] * value[0]
                real = pr if real is None else real + pr
                imag = pi if imag is None else imag + pi
            out.append((real, imag))
        result.append(out)
    return result


def map_half(function, half):
    return [[(function(v[0]), function(v[1])) for v in row] for row in half]


def load_link(get):
    return [[(get(a * 3 + b), get(9 + a * 3 + b)) for b in range(3)] for a in range(3)]


def load_spinor(ref):
    return [[(ref[s * 3 + c], ref[12 + s * 3 + c]) for c in range(3)] for s in range(4)]


def store_spinor(ref, field):
    for s in range(4):
        for c in range(3):
            ref[s * 3 + c] = field[s][c][0]
            ref[12 + s * 3 + c] = field[s][c][1]


def flat_half(half):
    return [half[s][c][part] for part in range(2) for s in range(2) for c in range(3)]


def unflat_half(flat):
    return [[(flat[s * 3 + c], flat[6 + s * 3 + c]) for c in range(3)] for s in range(2)]


def scaled(field, factor):
    return [[(factor * v[0], factor * v[1]) for v in row] for row in field]


def compact(ref, index, color, first):
    low = ref[index, :, 0:128]
    high = ref[index, :, 128:256]
    return jnp.where(first, low, high) if color == 0 else jnp.where(first, high, low)


def solve(rho_ref, w_ref, applied_ref, masked_ref, link):
    lane, time = lane_ids(), time_ids()
    inner = {X: lane % 8 != 7, Y: lane < 112, T: time != 7}
    for slot, direction in enumerate((X, Y, T)):
        for i in range(18):
            masked_ref[slot * 18 + i] = jnp.where(
                inner[direction], -0.5 * link(direction, i), 0.0
            )
    ahead = {
        X: lambda v: lanes_by(v, -1),
        Y: lambda v: lanes_by(v, -16),
        T: lambda v: times_by(v, -1),
    }
    behind = {
        X: lambda v: lanes_by(v, 1),
        Y: lambda v: lanes_by(v, 16),
        T: lambda v: times_by(v, 1),
    }
    left = (lane // 8) % 2 == 0

    def apply(field):
        total = scaled(field, DIAGONAL)
        for slot, direction in enumerate((X, Y, T)):
            matrix = load_link(lambda i: masked_ref[slot * 18 + i])
            half = map_half(ahead[direction], project(field, direction, -1))
            expand_into(total, color_apply(matrix, half, False), direction, -1)
            half = color_apply(matrix, project(field, direction, 1), True)
            expand_into(total, map_half(behind[direction], half), direction, 1)
        return total

    def weights(applied, rho):
        real, imag, square = None, None, None
        for s in range(4):
            for c in range(3):
                (ar, ai), (rr, ri) = applied[s][c], rho[s][c]
                pr = ar * rr + ai * ri
                pi = ar * ri - ai * rr
                ps = ar * ar + ai * ai
                real = pr if real is None else real + pr
                imag = pi if imag is None else imag + pi
                square = ps if square is None else square + ps
        sums = []
        for value in (real, imag, square):
            value = value + times_by(value, 4)
            value = value + times_by(value, 2)
            sums.append(value + times_by(value, 1))
        kind = time % 4
        rows = jnp.where(kind == 0, sums[0], jnp.where(kind == 1, sums[1], sums[2]))
        rows = jnp.where(left == (time < 4), rows, 0.0)
        means = jnp.sum(rows, axis=1, keepdims=True) / ENTRIES
        means = jnp.broadcast_to(means, TILE)
        one_on = times_by(means, -1)
        under = jnp.where(kind == 0, times_by(means, -2), one_on) + EPSILON
        ratio = means / under

        def at(row):
            near = jnp.broadcast_to(ratio[row : row + 1, :], TILE)
            far = jnp.broadcast_to(ratio[row + 4 : row + 5, :], TILE)
            return jnp.where(left, near, far)

        return at(0), at(1)

    def advance(weight, again):
        real, imag = weight
        for i in range(12):
            rr, ri = rho_ref[i], rho_ref[12 + i]
            ar, ai = applied_ref[i], applied_ref[12 + i]
            w_ref[i] = w_ref[i] + (real * rr - imag * ri)
            w_ref[12 + i] = w_ref[12 + i] + (real * ri + imag * rr)
            rho_ref[i] = rr - (real * ar - imag * ai)
            rho_ref[12 + i] = ri - (real * ai + imag * ar)
            if again is not None:
                br, bi = again[i // 3][i % 3]
                applied_ref[i] = ar - (real * br - imag * bi)
                applied_ref[12 + i] = ai - (real * bi + imag * br)

    def step(_, carry):
        applied = load_spinor(applied_ref)
        weight = weights(applied, load_spinor(rho_ref))
        advance(weight, apply(applied))
        return carry

    for i in range(24):
        w_ref[i] = jnp.zeros(TILE, F32)
    store_spinor(applied_ref, apply(load_spinor(rho_ref)))
    lax.fori_loop(0, NMR - 1, step, 0)
    advance(weights(load_spinor(applied_ref), load_spinor(rho_ref)), None)


def add_local_hops(total, half_w, link_to, link_from):
    lane = lane_ids()
    column = lane % 16

    def x_ahead(v):
        near = jnp.where(column == 7, lanes_by(v, -1), 0.0)
        return jnp.where(column == 15, lanes_by(v, 15), near)

    def x_behind(v):
        near = jnp.where(column == 8, lanes_by(v, 1), 0.0)
        return jnp.where(column == 0, lanes_by(v, -15), near)

    def y_ahead(v):
        return jnp.where(lane >= 112, lanes_by(v, -16), 0.0)

    def y_behind(v):
        return jnp.where(lane < 16, lanes_by(v, 16), 0.0)

    for direction, ahead, behind in ((X, x_ahead, x_behind), (Y, y_ahead, y_behind)):
        half = map_half(ahead, project(half_w, direction, -1))
        matrix = load_link(lambda i: link_to(direction, i))
        expand_into(total, color_apply(matrix, half, False), direction, -1)
        matrix = load_link(lambda i: link_from(direction, i))
        half = map_half(behind, color_apply(matrix, project(half_w, direction, 1), True))
        expand_into(total, half, direction, 1)


def outgoing(half_w, link_from, direction):
    matrix = load_link(lambda i: link_from(direction, i))
    ahead = color_apply(matrix, project(half_w, direction, 1), True)
    behind = project(half_w, direction, -1)
    return flat_half(ahead), flat_half(behind)


def store_pairs(even, ahead, behind, first_ref, second_ref):
    for i in range(len(ahead)):
        first_ref[i] = jnp.where(even, ahead[i], behind[i])
        second_ref[i] = jnp.where(even, behind[i], ahead[i])


def load_pairs(even, first, second):
    low = [jnp.where(even, b, a) for a, b in zip(first, second)]
    high = [jnp.where(even, a, b) for a, b in zip(first, second)]
    return low, high


def store_rows(ref, index, row):
    ref[index : index + 1, :] = row


def row_at(ref, time):
    here = time_ids() == time
    return unflat_half(
        [jnp.where(here, jnp.broadcast_to(ref[i : i + 1, :], TILE), 0.0) for i in range(12)]
    )


def store_faces(half_w, depth_half_w, link_from, t_refs, z_refs):
    ahead, behind = outgoing(depth_half_w, link_from, Z)
    store_pairs(is_even("gz"), ahead, behind, *z_refs)
    ahead, behind = outgoing(half_w, link_from, T)
    even = is_even("ta")[0:1, :]
    for i in range(12):
        low, high = behind[i][0:1, :], ahead[i][7:8, :]
        store_rows(t_refs[0], i, jnp.where(even, high, low))
        store_rows(t_refs[1], i, jnp.where(even, low, high))


def add_faces(total, link_to, t_refs, z_refs):
    low, high = load_pairs(
        is_even("gz"), [z_refs[0][i] for i in range(12)], [z_refs[1][i] for i in range(12)]
    )
    expand_into(total, unflat_half(low), Z, 1)
    matrix = load_link(lambda i: link_to(Z, i))
    expand_into(total, color_apply(matrix, unflat_half(high), False), Z, -1)
    time = time_ids()
    rows = [
        [jnp.broadcast_to(ref[i : i + 1, :], TILE) for i in range(12)] for ref in t_refs
    ]
    low, high = load_pairs(is_even("ta"), *rows)
    low = unflat_half([jnp.where(time == 0, v, 0.0) for v in low])
    high = unflat_half([jnp.where(time == 7, v, 0.0) for v in high])
    expand_into(total, low, T, 1)
    matrix = load_link(lambda i: link_to(T, i))
    expand_into(total, color_apply(matrix, high, False), T, -1)


def packed_lower(flat):
    low = time_ids() < 4
    return [jnp.where(low, flat[i + 6], times_by(flat[i], 4)) for i in range(6)]


def unpacked_lower(tiles):
    low = time_ids() < 4
    flat = [jnp.where(low, 0.0, v) for v in tiles]
    flat += [jnp.where(low, 0.0, times_by(v, 4)) for v in tiles]
    return unflat_half(flat)


def packed_split(flat):
    low = time_ids() < 4
    stay, move = [], []
    for i in range(6):
        turned = times_by(flat[i], 4)
        stay.append(jnp.where(low, turned, flat[i + 6]))
        move.append(jnp.where(low, flat[i + 6], turned))
    return stay, move


def join_split(low_tiles, high_tiles):
    low = time_ids() < 4
    flat = [jnp.where(low, a, b) for a, b in zip(low_tiles, high_tiles)]
    flat += [times_by(jnp.where(low, b, a), 4) for a, b in zip(low_tiles, high_tiles)]
    return unflat_half(flat)


def zero_spinor():
    zero = jnp.zeros(TILE, F32)
    return [[(zero, zero) for _ in range(3)] for _ in range(4)]


def masked_spinor(field, mask):
    return [[(jnp.where(mask, v[0], 0.0), jnp.where(mask, v[1], 0.0)) for v in row] for row in field]


def add_spinor(total, other):
    for s in range(4):
        for c in range(3):
            a, b = total[s][c], other[s][c]
            total[s][c] = (a[0] + b[0], a[1] + b[1])


def raw_links(links_ref):
    first = row_zero_first()
    return [
        lambda direction, i, color=color: compact(links_ref, direction * 18 + i, color, first)
        for color in range(2)
    ]


def fill_moved_links(moved_ref, links_ref, received_ref):
    first = row_zero_first()
    low = time_ids() < 4
    for i in range(72):
        zero = times_by(compact(links_ref, i, 0, first), 4)
        one = times_by(compact(links_ref, i, 1, first), 4)
        other = received_ref[i]
        moved_ref[i] = jnp.where(low, other, zero)
        moved_ref[72 + i] = jnp.where(low, times_by(other, 4), one)


def moved_links(moved_ref):
    return [
        lambda direction, i, color=color: moved_ref[72 * color + direction * 18 + i]
        for color in range(2)
    ]


def packed_upper(ref):
    low = time_ids() < 4
    return [jnp.where(low, times_by(ref[i], 4), ref[12 + i]) for i in range(12)]


def unpacked_upper(ref, base):
    return [ref[base + i] for i in range(12)] + [times_by(ref[base + i], 4) for i in range(12)]


def kernel_one(links_ref, source_ref, w_ref, rho_ref, other_ref, t0_ref, t1_ref, z0_ref, z1_ref,
               packed_ref, applied_ref, masked_ref):
    first = row_zero_first()
    link = raw_links(links_ref)
    for i in range(24):
        rho_ref[i] = compact(source_ref, i, 0, first)
        other_ref[i] = compact(source_ref, i, 1, first)
    solve(rho_ref, w_ref, applied_ref, masked_ref, link[0])
    half_w = scaled(load_spinor(w_ref), 0.5)
    store_faces(half_w, half_w, link[0], (t0_ref, t1_ref), (z0_ref, z1_ref))
    total = load_spinor(other_ref)
    add_local_hops(total, half_w, link[1], link[0])
    store_spinor(other_ref, total)
    low = time_ids() < 4
    for i in range(72):
        zero = compact(links_ref, i, 0, first)
        one = compact(links_ref, i, 1, first)
        packed_ref[i] = jnp.where(low, times_by(one, 4), zero)
    for i, tile in enumerate(packed_upper(rho_ref)):
        packed_ref[72 + i] = tile


def kernel_two(links_ref, rho_in, other_in, t0_in, t1_in, z0_in, z1_in,
               w_ref, rest_ref, rho_ref, send_ref, tb_ref, z0_ref, z1_ref,
               applied_ref, masked_ref):
    link = raw_links(links_ref)
    total = load_spinor(other_in)
    add_faces(total, link[1], (t0_in, t1_in), (z0_in, z1_in))
    store_spinor(rho_ref, total)
    solve(rho_ref, w_ref, applied_ref, masked_ref, link[1])
    half_w = scaled(load_spinor(w_ref), 0.5)
    ahead, behind = outgoing(half_w, link[1], Z)
    store_pairs(is_even("gz"), packed_lower(ahead), packed_lower(behind), z0_ref, z1_ref)
    behind = flat_half(project(half_w, T, -1))
    for i in range(12):
        store_rows(tb_ref, i, behind[i][0:1, :])
    total = load_spinor(rho_in)
    add_local_hops(total, half_w, link[0], link[1])
    store_spinor(rest_ref, total)
    for i, tile in enumerate(packed_upper(rho_ref) + packed_upper(w_ref)):
        send_ref[i] = tile


def kernel_three(links_ref, moved_in, rest_in, rho_in, tb_in, received, z0_in, z1_in,
                 w_ref, rho_ref, other_ref, t0_ref, t1_ref, z0_ref, z1_ref,
                 applied_ref, masked_ref, moved_ref):
    fill_moved_links(moved_ref, links_ref, moved_in)
    link = moved_links(moved_ref)
    time = time_ids()
    low = time < 4
    ones, zeros = unpacked_upper(received, 0), unpacked_upper(moved_in, 72)
    for i in range(24):
        rho_ref[i] = jnp.where(low, ones[i], times_by(rest_in[i], 4))
        other_ref[i] = jnp.where(low, zeros[i], times_by(rho_in[i], 4))
    came = [jnp.where(low, 0.5 * v, 0.0) for v in unpacked_upper(received, 12)]
    came = [[(came[s * 3 + c], came[12 + s * 3 + c]) for c in range(3)] for s in range(4)]
    total = load_spinor(rho_ref)
    lower, higher = load_pairs(
        is_even("gz"), [z0_in[i] for i in range(6)], [z1_in[i] for i in range(6)]
    )
    expand_into(total, unpacked_lower(lower), Z, 1)
    matrix = load_link(lambda i: link[0](Z, i))
    expand_into(total, color_apply(matrix, unpacked_lower(higher), False), Z, -1)
    matrix = load_link(lambda i: link[0](T, i))
    half = color_apply(matrix, project(came, T, 1), True)
    half = map_half(lambda v: jnp.where(time == 4, times_by(v, 1), 0.0), half)
    expand_into(total, half, T, 1)
    store_spinor(rho_ref, total)
    total = load_spinor(other_ref)
    matrix = load_link(lambda i: link[1](T, i))
    expand_into(total, color_apply(matrix, row_at(tb_in, 3), False), T, -1)
    store_spinor(other_ref, total)
    solve(rho_ref, w_ref, applied_ref, masked_ref, link[0])
    half_w = scaled(load_spinor(w_ref), 0.5)
    depth_half_w = came
    add_spinor(depth_half_w, half_w)
    store_faces(half_w, depth_half_w, link[0], (t0_ref, t1_ref), (z0_ref, z1_ref))
    total = load_spinor(other_ref)
    add_local_hops(total, depth_half_w, link[1], link[0])
    store_spinor(other_ref, total)


def kernel_four(links_ref, moved_in, w_in, rho_in, other_in, t0_in, t1_in, z0_in, z1_in,
                w_ref, rest_ref, rho_ref, send_ref, ta_ref, z0_ref, z1_ref, za_ref, zb_ref,
                applied_ref, masked_ref, moved_ref):
    fill_moved_links(moved_ref, links_ref, moved_in)
    link = moved_links(moved_ref)
    total = load_spinor(other_in)
    add_faces(total, link[1], (t0_in, t1_in), (z0_in, z1_in))
    store_spinor(rho_ref, total)
    solve(rho_ref, w_ref, applied_ref, masked_ref, link[1])
    half_w = scaled(load_spinor(w_ref), 0.5)
    ahead, behind = outgoing(half_w, link[1], Z)
    ahead, ahead_move = packed_split(ahead)
    behind, behind_move = packed_split(behind)
    store_pairs(is_even("gz"), ahead, behind, z0_ref, z1_ref)
    for i in range(6):
        za_ref[i] = ahead_move[i]
        zb_ref[i] = behind_move[i]
    matrix = load_link(lambda i: link[1](T, i))
    ahead = flat_half(color_apply(matrix, project(half_w, T, 1), True))
    for i in range(12):
        store_rows(ta_ref, i, ahead[i][7:8, :])
    total = load_spinor(rho_in)
    add_local_hops(total, half_w, link[0], link[1])
    store_spinor(rest_ref, total)
    low = time_ids() < 4
    for i in range(24):
        send_ref[i] = jnp.where(low, rho_ref[i], times_by(rest_ref[i], 4))
        send_ref[24 + i] = jnp.where(low, w_ref[i], times_by(w_in[i], 4))


def kernel_five(links_ref, w0_ref, w1_ref, x0_ref, x1_ref, rest_in, rho_in, ta_in, received,
                z0_in, z1_in, za_in, zb_in, solution_ref, residual_ref):
    link = raw_links(links_ref)
    first = row_zero_first()
    time = time_ids()
    low = time < 4

    def put(ref, i, zero, one):
        ref[i, :, 0:128] = jnp.where(first, zero, one)
        ref[i, :, 128:256] = jnp.where(first, one, zero)

    update = []
    for i in range(24):
        other = received[24 + i]
        zero = jnp.where(low, times_by(x0_ref[i], 4), times_by(other, 4))
        one = jnp.where(low, times_by(x1_ref[i], 4), other)
        put(solution_ref, i, w0_ref[i] + zero, w1_ref[i] + one)
        update.append(zero)
    lower, higher = load_pairs(
        is_even("gz"), [z0_in[i] for i in range(6)], [z1_in[i] for i in range(6)]
    )
    faces = zero_spinor()
    expand_into(faces, join_split(lower, [za_in[i] for i in range(6)]), Z, 1)
    matrix = load_link(lambda i: jnp.where(low, link[0](Z, i), link[1](Z, i)))
    half = join_split(higher, [zb_in[i] for i in range(6)])
    expand_into(faces, color_apply(matrix, half, False), Z, -1)
    zero, one = masked_spinor(faces, low), masked_spinor(faces, jnp.logical_not(low))
    update = [
        [(0.5 * update[s * 3 + c], 0.5 * update[12 + s * 3 + c]) for c in range(3)] for s in range(4)
    ]
    half = map_half(
        lambda v: jnp.where(time == 3, times_by(v, -1), 0.0), project(update, T, -1)
    )
    matrix = load_link(lambda i: link[0](T, i))
    expand_into(zero, color_apply(matrix, half, False), T, -1)
    expand_into(one, row_at(ta_in, 4), T, 1)
    for s in range(4):
        for c in range(3):
            for part in range(2):
                i = part * 12 + s * 3 + c
                other = received[i]
                base_zero = jnp.where(low, times_by(rest_in[i], 4), times_by(other, 4))
                base_one = jnp.where(low, times_by(rho_in[i], 4), other)
                put(residual_ref, i, base_zero + zero[s][c][part], base_one + one[s][c][part])


def call(kernel, shapes, operands, solver=False, moved=False, cost=3000000):
    scratch = []
    if solver:
        scratch = [pltpu.VMEM((24,) + TILE, F32), pltpu.VMEM((54,) + TILE, F32)]
    if moved:
        scratch.append(pltpu.VMEM((144,) + TILE, F32))
    vmem = pl.BlockSpec(memory_space=pltpu.VMEM)
    return pl.pallas_call(
        kernel,
        out_shape=[jax.ShapeDtypeStruct(shape, F32) for shape in shapes],
        in_specs=[vmem] * len(operands),
        out_specs=[vmem] * len(shapes),
        scratch_shapes=scratch,
        compiler_params=pltpu.CompilerParams(vmem_limit_bytes=12 << 20),
        cost_estimate=pl.CostEstimate(flops=cost, bytes_accessed=cost // 2, transcendentals=0),
    )(*operands)


def moved_to(value, time_steps, depth_steps):
    times, depths = lax.axis_size("ta"), lax.axis_size("gz")
    if depth_steps == 0:
        return lax.ppermute(value, "ta", [(i, (i + time_steps) % times) for i in range(times)])
    pairs = [
        (t * depths + g, (t + time_steps) % times * depths + (g + depth_steps) % depths)
        for t in range(times)
        for g in range(depths)
    ]
    return lax.ppermute(value, ("ta", "gz"), pairs)


def exchanged(value, axis, odd):
    count = lax.axis_size(axis)
    pairs = [(i, (i + (1 if i % 2 == odd else -1)) % count) for i in range(count)]
    return lax.ppermute(value, axis, pairs)


def exchange_faces(t0, t1, z0, z1):
    z0 = exchanged(z0, "gz", 0)
    t0 = exchanged(t0, "ta", 0)
    z1 = exchanged(z1, "gz", 1)
    t1 = exchanged(t1, "ta", 1)
    return [t0, t1, z0, z1]


def per_device(links, source):
    links = links.reshape((72, 8, 256))
    source = source.reshape((24, 8, 256))
    spinor, half, quarter, rows = (24,) + TILE, (12,) + TILE, (6,) + TILE, (12, 128)
    faces = [rows] * 2 + [half] * 2
    w0, rho0, other, *sent, packed = call(
        kernel_one, [spinor] * 3 + faces + [(84,) + TILE], [links, source], solver=True
    )
    moved = moved_to(packed, 1, 0)
    came = exchange_faces(*sent)
    w1, rest, rho1, send, tb, z0, z1 = call(
        kernel_two,
        [spinor] * 3 + [(24,) + TILE, rows, quarter, quarter],
        [links, rho0, other] + came,
        solver=True,
    )
    z0 = exchanged(z0, "gz", 0)
    z1 = exchanged(z1, "gz", 1)
    send = moved_to(send, 1, 0)
    x0, rho0, other, *sent = call(
        kernel_three,
        [spinor] * 3 + faces,
        [links, moved, rest, rho1, tb, send, z0, z1],
        solver=True,
        moved=True,
    )
    came = exchange_faces(*sent)
    x1, rest, rho1, send, ta, z0, z1, za, zb = call(
        kernel_four,
        [spinor] * 3 + [(48,) + TILE, rows] + [quarter] * 4,
        [links, moved, x0, rho0, other] + came,
        solver=True,
        moved=True,
    )
    z0 = exchanged(z0, "gz", 0)
    z1 = exchanged(z1, "gz", 1)
    send = moved_to(send, -1, 0)
    za = moved_to(za, -1, 1)
    zb = moved_to(zb, -1, -1)
    solution, residual = call(
        kernel_five,
        [(24, 8, 256)] * 2,
        [links, w0, w1, x0, x1, rest, rho1, ta, send, z0, z1, za, zb],
    )
    return solution.reshape((24, 1, 8, 256)), residual.reshape((24, 1, 8, 256))


def solution(mesh):
    in_specs = (P(None, None, "gz", "ta", None), P(None, "gz", "ta", None))
    out_specs = (P(None, "gz", "ta", None), P(None, "gz", "ta", None))
    return jax.shard_map(
        per_device, mesh=mesh, in_specs=in_specs, out_specs=out_specs, check_vma=False
    )
```

```python
import jax
import jax.numpy as jnp
from jax import lax
from jax.experimental import pallas as pl
from jax.experimental.pallas import tpu as pltpu
from jax.sharding import PartitionSpec as P


NMR = 4
DIAGONAL = 4.0 + 0.2
EPSILON = 1e-06
ENTRIES = 12 * 8 * 8 * 8
X, Y, Z, T = 0, 1, 2, 3
COLUMN = ((3, 2, 1, 0), (3, 2, 1, 0), (2, 3, 0, 1), (2, 3, 0, 1))
REAL = ((0, 0, 0, 0), (-1, 1, 1, -1), (0, 0, 0, 0), (1, 1, 1, 1))
IMAG = ((1, 1, -1, -1), (0, 0, 0, 0), (1, -1, -1, 1), (0, 0, 0, 0))
TILE = (8, 128)
F32 = jnp.float32


def lane_ids():
    return lax.broadcasted_iota(jnp.int32, TILE, 1)


def time_ids():
    return lax.broadcasted_iota(jnp.int32, TILE, 0)


def my_parity():
    return (lax.axis_index("gz") + lax.axis_index("ta")) % 2


def row_zero_first():
    return (lane_ids() // 8) % 2 == my_parity()


def is_even(axis):
    return (lane_ids() * 0 + lax.axis_index(axis)) % 2 == 0


def lanes_by(value, steps):
    return pltpu.roll(value, steps % 128, 1)


def times_by(value, steps):
    return pltpu.roll(value, steps % 8, 0)


def add_gamma(base, orientation, direction, row, value):
    real = orientation * REAL[direction][row]
    imag = orientation * IMAG[direction][row]
    if real > 0:
        return (base[0] + value[0], base[1] + value[1])
    if real < 0:
        return (base[0] - value[0], base[1] - value[1])
    if imag > 0:
        return (base[0] - value[1], base[1] + value[0])
    return (base[0] + value[1], base[1] - value[0])


def project(field, direction, orientation):
    return [
        [
            add_gamma(
                field[row][color], orientation, direction, row, field[COLUMN[direction][row]][color]
            )
            for color in range(3)
        ]
        for row in range(2)
    ]


def expand_into(total, half, direction, orientation):
    for row in range(4):
        for color in range(3):
            if row < 2:
                base, value = total[row][color], half[row][color]
                total[row][color] = (base[0] + value[0], base[1] + value[1])
            else:
                total[row][color] = add_gamma(
                    total[row][color],
                    orientation,
                    direction,
                    row,
                    half[COLUMN[direction][row]][color],
                )


def color_apply(link, half, adjoint):
    result = []
    for row in range(2):
        out = []
        for a in range(3):
            real, imag = None, None
            for b in range(3):
                value = half[row][b]
                entry = link[b][a] if adjoint else link[a][b]
                if adjoint:
                    pr = entry[0] * value[0] + entry[1] * value[1]
                    pi = entry[0] * value[1] - entry[1] * value[0]
                else:
                    pr = entry[0] * value[0] - entry[1] * value[1]
                    pi = entry[0] * value[1] + entry[1] * value[0]
                real = pr if real is None else real + pr
                imag = pi if imag is None else imag + pi
            out.append((real, imag))
        result.append(out)
    return result


def map_half(function, half):
    return [[(function(v[0]), function(v[1])) for v in row] for row in half]


def load_link(get):
    return [[(get(a * 3 + b), get(9 + a * 3 + b)) for b in range(3)] for a in range(3)]


def load_spinor(ref):
    return [[(ref[s * 3 + c], ref[12 + s * 3 + c]) for c in range(3)] for s in range(4)]


def store_spinor(ref, field):
    for s in range(4):
        for c in range(3):
            ref[s * 3 + c] = field[s][c][0]
            ref[12 + s * 3 + c] = field[s][c][1]


def flat_half(half):
    return [half[s][c][part] for part in range(2) for s in range(2) for c in range(3)]


def unflat_half(flat):
    return [[(flat[s * 3 + c], flat[6 + s * 3 + c]) for c in range(3)] for s in range(2)]


def scaled(field, factor):
    return [[(factor * v[0], factor * v[1]) for v in row] for row in field]


def compact(ref, index, color, first):
    low = ref[index, :, 0:128]
    high = ref[index, :, 128:256]
    return jnp.where(first, low, high) if color == 0 else jnp.where(first, high, low)


def solve(rho_ref, w_ref, applied_ref, masked_ref, link):
    lane, time = lane_ids(), time_ids()
    inner = {X: lane % 8 != 7, Y: lane < 112, T: time != 7}
    for slot, direction in enumerate((X, Y, T)):
        for i in range(18):
            masked_ref[slot * 18 + i] = jnp.where(
                inner[direction], -0.5 * link(direction, i), 0.0
            )
    ahead = {
        X: lambda v: lanes_by(v, -1),
        Y: lambda v: lanes_by(v, -16),
        T: lambda v: times_by(v, -1),
    }
    behind = {
        X: lambda v: lanes_by(v, 1),
        Y: lambda v: lanes_by(v, 16),
        T: lambda v: times_by(v, 1),
    }
    left = (lane // 8) % 2 == 0

    def apply(field):
        total = scaled(field, DIAGONAL)
        for slot, direction in enumerate((X, Y, T)):
            matrix = load_link(lambda i: masked_ref[slot * 18 + i])
            half = map_half(ahead[direction], project(field, direction, -1))
            expand_into(total, color_apply(matrix, half, False), direction, -1)
            half = color_apply(matrix, project(field, direction, 1), True)
            expand_into(total, map_half(behind[direction], half), direction, 1)
        return total

    def weights(applied, rho):
        real, imag, square = None, None, None
        for s in range(4):
            for c in range(3):
                (ar, ai), (rr, ri) = applied[s][c], rho[s][c]
                pr = ar * rr + ai * ri
                pi = ar * ri - ai * rr
                ps = ar * ar + ai * ai
                real = pr if real is None else real + pr
                imag = pi if imag is None else imag + pi
                square = ps if square is None else square + ps
        sums = []
        for value in (real, imag, square):
            value = value + times_by(value, 4)
            value = value + times_by(value, 2)
            sums.append(value + times_by(value, 1))
        kind = time % 4
        rows = jnp.where(kind == 0, sums[0], jnp.where(kind == 1, sums[1], sums[2]))
        rows = jnp.where(left == (time < 4), rows, 0.0)
        means = jnp.sum(rows, axis=1, keepdims=True) / ENTRIES
        means = jnp.broadcast_to(means, TILE)
        one_on = times_by(means, -1)
        under = jnp.where(kind == 0, times_by(means, -2), one_on) + EPSILON
        ratio = means / under

        def at(row):
            near = jnp.broadcast_to(ratio[row : row + 1, :], TILE)
            far = jnp.broadcast_to(ratio[row + 4 : row + 5, :], TILE)
            return jnp.where(left, near, far)

        return at(0), at(1)

    def advance(weight, again):
        real, imag = weight
        for i in range(12):
            rr, ri = rho_ref[i], rho_ref[12 + i]
            ar, ai = applied_ref[i], applied_ref[12 + i]
            w_ref[i] = w_ref[i] + (real * rr - imag * ri)
            w_ref[12 + i] = w_ref[12 + i] + (real * ri + imag * rr)
            rho_ref[i] = rr - (real * ar - imag * ai)
            rho_ref[12 + i] = ri - (real * ai + imag * ar)
            if again is not None:
                br, bi = again[i // 3][i % 3]
                applied_ref[i] = ar - (real * br - imag * bi)
                applied_ref[12 + i] = ai - (real * bi + imag * br)

    def step(_, carry):
        applied = load_spinor(applied_ref)
        weight = weights(applied, load_spinor(rho_ref))
        advance(weight, apply(applied))
        return carry

    for i in range(24):
        w_ref[i] = jnp.zeros(TILE, F32)
    store_spinor(applied_ref, apply(load_spinor(rho_ref)))
    lax.fori_loop(0, NMR - 1, step, 0)
    advance(weights(load_spinor(applied_ref), load_spinor(rho_ref)), None)


def add_local_hops(total, half_w, link_to, link_from):
    lane = lane_ids()
    column = lane % 16

    def x_ahead(v):
        near = jnp.where(column == 7, lanes_by(v, -1), 0.0)
        return jnp.where(column == 15, lanes_by(v, 15), near)

    def x_behind(v):
        near = jnp.where(column == 8, lanes_by(v, 1), 0.0)
        return jnp.where(column == 0, lanes_by(v, -15), near)

    def y_ahead(v):
        return jnp.where(lane >= 112, lanes_by(v, -16), 0.0)

    def y_behind(v):
        return jnp.where(lane < 16, lanes_by(v, 16), 0.0)

    for direction, ahead, behind in ((X, x_ahead, x_behind), (Y, y_ahead, y_behind)):
        half = map_half(ahead, project(half_w, direction, -1))
        matrix = load_link(lambda i: link_to(direction, i))
        expand_into(total, color_apply(matrix, half, False), direction, -1)
        matrix = load_link(lambda i: link_from(direction, i))
        half = map_half(behind, color_apply(matrix, project(half_w, direction, 1), True))
        expand_into(total, half, direction, 1)


def outgoing(half_w, link_from, direction):
    matrix = load_link(lambda i: link_from(direction, i))
    ahead = color_apply(matrix, project(half_w, direction, 1), True)
    behind = project(half_w, direction, -1)
    return flat_half(ahead), flat_half(behind)


def store_pairs(even, ahead, behind, first_ref, second_ref):
    for i in range(len(ahead)):
        first_ref[i] = jnp.where(even, ahead[i], behind[i])
        second_ref[i] = jnp.where(even, behind[i], ahead[i])


def load_pairs(even, first, second):
    low = [jnp.where(even, b, a) for a, b in zip(first, second)]
    high = [jnp.where(even, a, b) for a, b in zip(first, second)]
    return low, high


def store_rows(ref, index, row):
    ref[index : index + 1, :] = row


def row_at(ref, time):
    here = time_ids() == time
    return unflat_half(
        [jnp.where(here, jnp.broadcast_to(ref[i : i + 1, :], TILE), 0.0) for i in range(12)]
    )


def store_faces(half_w, depth_half_w, link_from, t_refs, z_refs):
    ahead, behind = outgoing(depth_half_w, link_from, Z)
    store_pairs(is_even("gz"), ahead, behind, *z_refs)
    ahead, behind = outgoing(half_w, link_from, T)
    even = is_even("ta")[0:1, :]
    for i in range(12):
        low, high = behind[i][0:1, :], ahead[i][7:8, :]
        store_rows(t_refs[0], i, jnp.where(even, high, low))
        store_rows(t_refs[1], i, jnp.where(even, low, high))


def add_faces(total, link_to, t_refs, z_refs):
    low, high = load_pairs(
        is_even("gz"), [z_refs[0][i] for i in range(12)], [z_refs[1][i] for i in range(12)]
    )
    expand_into(total, unflat_half(low), Z, 1)
    matrix = load_link(lambda i: link_to(Z, i))
    expand_into(total, color_apply(matrix, unflat_half(high), False), Z, -1)
    time = time_ids()
    rows = [
        [jnp.broadcast_to(ref[i : i + 1, :], TILE) for i in range(12)] for ref in t_refs
    ]
    low, high = load_pairs(is_even("ta"), *rows)
    low = unflat_half([jnp.where(time == 0, v, 0.0) for v in low])
    high = unflat_half([jnp.where(time == 7, v, 0.0) for v in high])
    expand_into(total, low, T, 1)
    matrix = load_link(lambda i: link_to(T, i))
    expand_into(total, color_apply(matrix, high, False), T, -1)


def packed_lower(flat):
    low = time_ids() < 4
    return [jnp.where(low, flat[i + 6], times_by(flat[i], 4)) for i in range(6)]


def unpacked_lower(tiles):
    low = time_ids() < 4
    flat = [jnp.where(low, 0.0, v) for v in tiles]
    flat += [jnp.where(low, 0.0, times_by(v, 4)) for v in tiles]
    return unflat_half(flat)


def packed_split(flat):
    low = time_ids() < 4
    stay, move = [], []
    for i in range(6):
        turned = times_by(flat[i], 4)
        stay.append(jnp.where(low, turned, flat[i + 6]))
        move.append(jnp.where(low, flat[i + 6], turned))
    return stay, move


def join_split(low_tiles, high_tiles):
    low = time_ids() < 4
    flat = [jnp.where(low, a, b) for a, b in zip(low_tiles, high_tiles)]
    flat += [times_by(jnp.where(low, b, a), 4) for a, b in zip(low_tiles, high_tiles)]
    return unflat_half(flat)


def zero_spinor():
    zero = jnp.zeros(TILE, F32)
    return [[(zero, zero) for _ in range(3)] for _ in range(4)]


def masked_spinor(field, mask):
    return [[(jnp.where(mask, v[0], 0.0), jnp.where(mask, v[1], 0.0)) for v in row] for row in field]


def add_spinor(total, other):
    for s in range(4):
        for c in range(3):
            a, b = total[s][c], other[s][c]
            total[s][c] = (a[0] + b[0], a[1] + b[1])


def raw_links(links_ref):
    first = row_zero_first()
    return [
        lambda direction, i, color=color: compact(links_ref, direction * 18 + i, color, first)
        for color in range(2)
    ]


def fill_moved_links(moved_ref, links_ref, received_ref):
    first = row_zero_first()
    low = time_ids() < 4
    for i in range(72):
        zero = times_by(compact(links_ref, i, 0, first), 4)
        one = times_by(compact(links_ref, i, 1, first), 4)
        other = received_ref[i]
        moved_ref[i] = jnp.where(low, other, zero)
        moved_ref[72 + i] = jnp.where(low, times_by(other, 4), one)


def moved_links(moved_ref):
    return [
        lambda direction, i, color=color: moved_ref[72 * color + direction * 18 + i]
        for color in range(2)
    ]


def packed_upper(ref):
    low = time_ids() < 4
    return [jnp.where(low, times_by(ref[i], 4), ref[12 + i]) for i in range(12)]


def unpacked_upper(ref, base):
    return [ref[base + i] for i in range(12)] + [times_by(ref[base + i], 4) for i in range(12)]


def kernel_one(links_hbm, source_hbm, w_ref, rho_ref, other_ref, t0_ref, t1_ref, z0_ref, z1_ref,
               packed_ref, links_ref, applied_ref, masked_ref, source_ref, arrived):
    first = row_zero_first()
    link = raw_links(links_ref)
    copies = [
        pltpu.make_async_copy(
            links_hbm.at[direction * 18 : direction * 18 + 18],
            links_ref.at[direction * 18 : direction * 18 + 18],
            arrived.at[direction],
        )
        for direction in range(4)
    ]
    source_copy = pltpu.make_async_copy(source_hbm, source_ref, arrived.at[4])
    source_copy.start()
    for direction in (X, Y, T, Z):
        copies[direction].start()
    source_copy.wait()
    for i in range(24):
        rho_ref[i] = compact(source_ref, i, 0, first)
        other_ref[i] = compact(source_ref, i, 1, first)
    for direction in (X, Y, T):
        copies[direction].wait()
    solve(rho_ref, w_ref, applied_ref, masked_ref, link[0])
    copies[Z].wait()
    half_w = scaled(load_spinor(w_ref), 0.5)
    store_faces(half_w, half_w, link[0], (t0_ref, t1_ref), (z0_ref, z1_ref))
    total = load_spinor(other_ref)
    add_local_hops(total, half_w, link[1], link[0])
    store_spinor(other_ref, total)
    low = time_ids() < 4
    for i in range(72):
        zero = compact(links_ref, i, 0, first)
        one = compact(links_ref, i, 1, first)
        packed_ref[i] = jnp.where(low, times_by(one, 4), zero)
    for i, tile in enumerate(packed_upper(rho_ref)):
        packed_ref[72 + i] = tile


def kernel_two(links_ref, rho_in, other_in, t0_in, t1_in, z0_in, z1_in,
               w_ref, rest_ref, rho_ref, send_ref, tb_ref, z0_ref, z1_ref,
               applied_ref, masked_ref):
    link = raw_links(links_ref)
    total = load_spinor(other_in)
    add_faces(total, link[1], (t0_in, t1_in), (z0_in, z1_in))
    store_spinor(rho_ref, total)
    solve(rho_ref, w_ref, applied_ref, masked_ref, link[1])
    half_w = scaled(load_spinor(w_ref), 0.5)
    ahead, behind = outgoing(half_w, link[1], Z)
    store_pairs(is_even("gz"), packed_lower(ahead), packed_lower(behind), z0_ref, z1_ref)
    behind = flat_half(project(half_w, T, -1))
    for i in range(12):
        store_rows(tb_ref, i, behind[i][0:1, :])
    total = load_spinor(rho_in)
    add_local_hops(total, half_w, link[0], link[1])
    store_spinor(rest_ref, total)
    for i, tile in enumerate(packed_upper(rho_ref) + packed_upper(w_ref)):
        send_ref[i] = tile


def kernel_three(links_ref, moved_in, rest_in, rho_in, tb_in, received, z0_in, z1_in,
                 w_ref, rho_ref, other_ref, t0_ref, t1_ref, z0_ref, z1_ref,
                 applied_ref, masked_ref, moved_ref):
    fill_moved_links(moved_ref, links_ref, moved_in)
    link = moved_links(moved_ref)
    time = time_ids()
    low = time < 4
    ones, zeros = unpacked_upper(received, 0), unpacked_upper(moved_in, 72)
    for i in range(24):
        rho_ref[i] = jnp.where(low, ones[i], times_by(rest_in[i], 4))
        other_ref[i] = jnp.where(low, zeros[i], times_by(rho_in[i], 4))
    came = [jnp.where(low, 0.5 * v, 0.0) for v in unpacked_upper(received, 12)]
    came = [[(came[s * 3 + c], came[12 + s * 3 + c]) for c in range(3)] for s in range(4)]
    total = load_spinor(rho_ref)
    lower, higher = load_pairs(
        is_even("gz"), [z0_in[i] for i in range(6)], [z1_in[i] for i in range(6)]
    )
    expand_into(total, unpacked_lower(lower), Z, 1)
    matrix = load_link(lambda i: link[0](Z, i))
    expand_into(total, color_apply(matrix, unpacked_lower(higher), False), Z, -1)
    matrix = load_link(lambda i: link[0](T, i))
    half = color_apply(matrix, project(came, T, 1), True)
    half = map_half(lambda v: jnp.where(time == 4, times_by(v, 1), 0.0), half)
    expand_into(total, half, T, 1)
    store_spinor(rho_ref, total)
    total = load_spinor(other_ref)
    matrix = load_link(lambda i: link[1](T, i))
    expand_into(total, color_apply(matrix, row_at(tb_in, 3), False), T, -1)
    store_spinor(other_ref, total)
    solve(rho_ref, w_ref, applied_ref, masked_ref, link[0])
    half_w = scaled(load_spinor(w_ref), 0.5)
    depth_half_w = came
    add_spinor(depth_half_w, half_w)
    store_faces(half_w, depth_half_w, link[0], (t0_ref, t1_ref), (z0_ref, z1_ref))
    total = load_spinor(other_ref)
    add_local_hops(total, depth_half_w, link[1], link[0])
    store_spinor(other_ref, total)


def kernel_four(links_ref, moved_in, w_in, rho_in, other_in, t0_in, t1_in, z0_in, z1_in,
                w_ref, rest_ref, rho_ref, send_ref, ta_ref, z0_ref, z1_ref, za_ref, zb_ref,
                applied_ref, masked_ref, moved_ref):
    fill_moved_links(moved_ref, links_ref, moved_in)
    link = moved_links(moved_ref)
    total = load_spinor(other_in)
    add_faces(total, link[1], (t0_in, t1_in), (z0_in, z1_in))
    store_spinor(rho_ref, total)
    solve(rho_ref, w_ref, applied_ref, masked_ref, link[1])
    half_w = scaled(load_spinor(w_ref), 0.5)
    ahead, behind = outgoing(half_w, link[1], Z)
    ahead, ahead_move = packed_split(ahead)
    behind, behind_move = packed_split(behind)
    store_pairs(is_even("gz"), ahead, behind, z0_ref, z1_ref)
    for i in range(6):
        za_ref[i] = ahead_move[i]
        zb_ref[i] = behind_move[i]
    matrix = load_link(lambda i: link[1](T, i))
    ahead = flat_half(color_apply(matrix, project(half_w, T, 1), True))
    for i in range(12):
        store_rows(ta_ref, i, ahead[i][7:8, :])
    total = load_spinor(rho_in)
    add_local_hops(total, half_w, link[0], link[1])
    store_spinor(rest_ref, total)
    low = time_ids() < 4
    for i in range(24):
        send_ref[i] = jnp.where(low, rho_ref[i], times_by(rest_ref[i], 4))
        send_ref[24 + i] = jnp.where(low, w_ref[i], times_by(w_in[i], 4))


def kernel_five(links_ref, w0_ref, w1_ref, x0_ref, x1_ref, rest_in, rho_in, ta_in, received,
                z0_in, z1_in, za_in, zb_in, solution_ref, residual_ref):
    link = raw_links(links_ref)
    first = row_zero_first()
    time = time_ids()
    low = time < 4

    def put(ref, i, zero, one):
        ref[i, :, 0:128] = jnp.where(first, zero, one)
        ref[i, :, 128:256] = jnp.where(first, one, zero)

    update = []
    for i in range(24):
        other = received[24 + i]
        zero = jnp.where(low, times_by(x0_ref[i], 4), times_by(other, 4))
        one = jnp.where(low, times_by(x1_ref[i], 4), other)
        put(solution_ref, i, w0_ref[i] + zero, w1_ref[i] + one)
        update.append(zero)
    lower, higher = load_pairs(
        is_even("gz"), [z0_in[i] for i in range(6)], [z1_in[i] for i in range(6)]
    )
    faces = zero_spinor()
    expand_into(faces, join_split(lower, [za_in[i] for i in range(6)]), Z, 1)
    matrix = load_link(lambda i: jnp.where(low, link[0](Z, i), link[1](Z, i)))
    half = join_split(higher, [zb_in[i] for i in range(6)])
    expand_into(faces, color_apply(matrix, half, False), Z, -1)
    zero, one = masked_spinor(faces, low), masked_spinor(faces, jnp.logical_not(low))
    update = [
        [(0.5 * update[s * 3 + c], 0.5 * update[12 + s * 3 + c]) for c in range(3)] for s in range(4)
    ]
    half = map_half(
        lambda v: jnp.where(time == 3, times_by(v, -1), 0.0), project(update, T, -1)
    )
    matrix = load_link(lambda i: link[0](T, i))
    expand_into(zero, color_apply(matrix, half, False), T, -1)
    expand_into(one, row_at(ta_in, 4), T, 1)
    for s in range(4):
        for c in range(3):
            for part in range(2):
                i = part * 12 + s * 3 + c
                other = received[i]
                base_zero = jnp.where(low, times_by(rest_in[i], 4), times_by(other, 4))
                base_one = jnp.where(low, times_by(rho_in[i], 4), other)
                put(residual_ref, i, base_zero + zero[s][c][part], base_one + one[s][c][part])


def call(kernel, shapes, operands, solver=False, moved=False, fetch=False, cost=3000000):
    scratch = []
    if solver:
        scratch = [pltpu.VMEM((24,) + TILE, F32), pltpu.VMEM((54,) + TILE, F32)]
    if moved:
        scratch.append(pltpu.VMEM((144,) + TILE, F32))
    if fetch:
        operands = [pltpu.with_memory_space_constraint(v, pltpu.HBM) for v in operands]
        scratch.append(pltpu.VMEM((24, 8, 256), F32))
        scratch.append(pltpu.SemaphoreType.DMA((5,)))
    vmem = pl.BlockSpec(memory_space=pltpu.VMEM)
    place = pl.BlockSpec(memory_space=pltpu.HBM) if fetch else vmem
    return pl.pallas_call(
        kernel,
        out_shape=[jax.ShapeDtypeStruct(shape, F32) for shape in shapes],
        in_specs=[place] * len(operands),
        out_specs=[vmem] * len(shapes),
        scratch_shapes=scratch,
        compiler_params=pltpu.CompilerParams(vmem_limit_bytes=12 << 20),
        cost_estimate=pl.CostEstimate(flops=cost, bytes_accessed=cost // 2, transcendentals=0),
    )(*operands)


def moved_to(value, time_steps, depth_steps):
    times, depths = lax.axis_size("ta"), lax.axis_size("gz")
    if depth_steps == 0:
        return lax.ppermute(value, "ta", [(i, (i + time_steps) % times) for i in range(times)])
    pairs = [
        (t * depths + g, (t + time_steps) % times * depths + (g + depth_steps) % depths)
        for t in range(times)
        for g in range(depths)
    ]
    return lax.ppermute(value, ("ta", "gz"), pairs)


def exchanged(value, axis, odd):
    count = lax.axis_size(axis)
    pairs = [(i, (i + (1 if i % 2 == odd else -1)) % count) for i in range(count)]
    return lax.ppermute(value, axis, pairs)


def exchange_faces(t0, t1, z0, z1):
    z0 = exchanged(z0, "gz", 0)
    t0 = exchanged(t0, "ta", 0)
    z1 = exchanged(z1, "gz", 1)
    t1 = exchanged(t1, "ta", 1)
    return [t0, t1, z0, z1]


def per_device(links, source):
    links = links.reshape((72, 8, 256))
    source = source.reshape((24, 8, 256))
    spinor, half, quarter, rows = (24,) + TILE, (12,) + TILE, (6,) + TILE, (12, 128)
    faces = [rows] * 2 + [half] * 2
    w0, rho0, other, *sent, packed, links = call(
        kernel_one,
        [spinor] * 3 + faces + [(84,) + TILE, (72, 8, 256)],
        [links, source],
        solver=True,
        fetch=True,
    )
    moved = moved_to(packed, 1, 0)
    came = exchange_faces(*sent)
    w1, rest, rho1, send, tb, z0, z1 = call(
        kernel_two,
        [spinor] * 3 + [(24,) + TILE, rows, quarter, quarter],
        [links, rho0, other] + came,
        solver=True,
    )
    z0 = exchanged(z0, "gz", 0)
    z1 = exchanged(z1, "gz", 1)
    send = moved_to(send, 1, 0)
    x0, rho0, other, *sent = call(
        kernel_three,
        [spinor] * 3 + faces,
        [links, moved, rest, rho1, tb, send, z0, z1],
        solver=True,
        moved=True,
    )
    came = exchange_faces(*sent)
    x1, rest, rho1, send, ta, z0, z1, za, zb = call(
        kernel_four,
        [spinor] * 3 + [(48,) + TILE, rows] + [quarter] * 4,
        [links, moved, x0, rho0, other] + came,
        solver=True,
        moved=True,
    )
    z0 = exchanged(z0, "gz", 0)
    z1 = exchanged(z1, "gz", 1)
    send = moved_to(send, -1, 0)
    za = moved_to(za, -1, 1)
    zb = moved_to(zb, -1, -1)
    solution, residual = call(
        kernel_five,
        [(24, 8, 256)] * 2,
        [links, w0, w1, x0, x1, rest, rho1, ta, send, z0, z1, za, zb],
    )
    return solution.reshape((24, 1, 8, 256)), residual.reshape((24, 1, 8, 256))


def solution(mesh):
    in_specs = (P(None, None, "gz", "ta", None), P(None, "gz", "ta", None))
    out_specs = (P(None, "gz", "ta", None), P(None, "gz", "ta", None))
    return jax.shard_map(
        per_device, mesh=mesh, in_specs=in_specs, out_specs=out_specs, check_vma=False
    )
```

```python
import jax
import jax.numpy as jnp
from jax import lax
from jax.experimental import pallas as pl
from jax.experimental.pallas import tpu as pltpu
from jax.sharding import PartitionSpec as P


NMR = 4
DIAGONAL = 4.0 + 0.2
EPSILON = 1e-06
ENTRIES = 12 * 8 * 8 * 8
X, Y, Z, T = 0, 1, 2, 3
COLUMN = ((3, 2, 1, 0), (3, 2, 1, 0), (2, 3, 0, 1), (2, 3, 0, 1))
REAL = ((0, 0, 0, 0), (-1, 1, 1, -1), (0, 0, 0, 0), (1, 1, 1, 1))
IMAG = ((1, 1, -1, -1), (0, 0, 0, 0), (1, -1, -1, 1), (0, 0, 0, 0))
TILE = (8, 128)
F32 = jnp.float32


def lane_ids():
    return lax.broadcasted_iota(jnp.int32, TILE, 1)


def time_ids():
    return lax.broadcasted_iota(jnp.int32, TILE, 0)


def my_parity():
    return (lax.axis_index("gz") + lax.axis_index("ta")) % 2


def row_zero_first():
    return (lane_ids() // 8) % 2 == my_parity()


def is_even(axis):
    return (lane_ids() * 0 + lax.axis_index(axis)) % 2 == 0


def lanes_by(value, steps):
    return pltpu.roll(value, steps % 128, 1)


def times_by(value, steps):
    return pltpu.roll(value, steps % 8, 0)


def add_gamma(base, orientation, direction, row, value):
    real = orientation * REAL[direction][row]
    imag = orientation * IMAG[direction][row]
    if real > 0:
        return (base[0] + value[0], base[1] + value[1])
    if real < 0:
        return (base[0] - value[0], base[1] - value[1])
    if imag > 0:
        return (base[0] - value[1], base[1] + value[0])
    return (base[0] + value[1], base[1] - value[0])


def project(field, direction, orientation):
    return [
        [
            add_gamma(
                field[row][color], orientation, direction, row, field[COLUMN[direction][row]][color]
            )
            for color in range(3)
        ]
        for row in range(2)
    ]


def expand_into(total, half, direction, orientation):
    for row in range(4):
        for color in range(3):
            if row < 2:
                base, value = total[row][color], half[row][color]
                total[row][color] = (base[0] + value[0], base[1] + value[1])
            else:
                total[row][color] = add_gamma(
                    total[row][color],
                    orientation,
                    direction,
                    row,
                    half[COLUMN[direction][row]][color],
                )


def color_apply(link, half, adjoint):
    result = []
    for row in range(2):
        out = []
        for a in range(3):
            real, imag = None, None
            for b in range(3):
                value = half[row][b]
                entry = link[b][a] if adjoint else link[a][b]
                if adjoint:
                    pr = entry[0] * value[0] + entry[1] * value[1]
                    pi = entry[0] * value[1] - entry[1] * value[0]
                else:
                    pr = entry[0] * value[0] - entry[1] * value[1]
                    pi = entry[0] * value[1] + entry[1] * value[0]
                real = pr if real is None else real + pr
                imag = pi if imag is None else imag + pi
            out.append((real, imag))
        result.append(out)
    return result


def map_half(function, half):
    return [[(function(v[0]), function(v[1])) for v in row] for row in half]


def load_link(get):
    return [[(get(a * 3 + b), get(9 + a * 3 + b)) for b in range(3)] for a in range(3)]


def load_spinor(ref):
    return [[(ref[s * 3 + c], ref[12 + s * 3 + c]) for c in range(3)] for s in range(4)]


def store_spinor(ref, field):
    for s in range(4):
        for c in range(3):
            ref[s * 3 + c] = field[s][c][0]
            ref[12 + s * 3 + c] = field[s][c][1]


def flat_half(half):
    return [half[s][c][part] for part in range(2) for s in range(2) for c in range(3)]


def unflat_half(flat):
    return [[(flat[s * 3 + c], flat[6 + s * 3 + c]) for c in range(3)] for s in range(2)]


def scaled(field, factor):
    return [[(factor * v[0], factor * v[1]) for v in row] for row in field]


def compact(ref, index, color, first):
    low = ref[index, :, 0:128]
    high = ref[index, :, 128:256]
    return jnp.where(first, low, high) if color == 0 else jnp.where(first, high, low)


def solve(rho_ref, w_ref, applied_ref, masked_ref, link):
    lane, time = lane_ids(), time_ids()
    inner = {X: lane % 8 != 7, Y: lane < 112, T: time != 7}
    for slot, direction in enumerate((X, Y, T)):
        for i in range(18):
            masked_ref[slot * 18 + i] = jnp.where(
                inner[direction], -0.5 * link(direction, i), 0.0
            )
    ahead = {
        X: lambda v: lanes_by(v, -1),
        Y: lambda v: lanes_by(v, -16),
        T: lambda v: times_by(v, -1),
    }
    behind = {
        X: lambda v: lanes_by(v, 1),
        Y: lambda v: lanes_by(v, 16),
        T: lambda v: times_by(v, 1),
    }
    left = (lane // 8) % 2 == 0

    def apply(field):
        total = scaled(field, DIAGONAL)
        for slot, direction in enumerate((X, Y, T)):
            matrix = load_link(lambda i: masked_ref[slot * 18 + i])
            half = map_half(ahead[direction], project(field, direction, -1))
            expand_into(total, color_apply(matrix, half, False), direction, -1)
            half = color_apply(matrix, project(field, direction, 1), True)
            expand_into(total, map_half(behind[direction], half), direction, 1)
        return total

    def weights(applied, rho):
        real, imag, square = None, None, None
        for s in range(4):
            for c in range(3):
                (ar, ai), (rr, ri) = applied[s][c], rho[s][c]
                pr = ar * rr + ai * ri
                pi = ar * ri - ai * rr
                ps = ar * ar + ai * ai
                real = pr if real is None else real + pr
                imag = pi if imag is None else imag + pi
                square = ps if square is None else square + ps
        sums = []
        for value in (real, imag, square):
            value = value + times_by(value, 4)
            value = value + times_by(value, 2)
            sums.append(value + times_by(value, 1))
        kind = time % 4
        rows = jnp.where(kind == 0, sums[0], jnp.where(kind == 1, sums[1], sums[2]))
        rows = jnp.where(left == (time < 4), rows, 0.0)
        means = jnp.sum(rows, axis=1, keepdims=True) / ENTRIES
        means = jnp.broadcast_to(means, TILE)
        one_on = times_by(means, -1)
        under = jnp.where(kind == 0, times_by(means, -2), one_on) + EPSILON
        ratio = means / under

        def at(row):
            near = jnp.broadcast_to(ratio[row : row + 1, :], TILE)
            far = jnp.broadcast_to(ratio[row + 4 : row + 5, :], TILE)
            return jnp.where(left, near, far)

        return at(0), at(1)

    def advance(weight, again):
        real, imag = weight
        for i in range(12):
            rr, ri = rho_ref[i], rho_ref[12 + i]
            ar, ai = applied_ref[i], applied_ref[12 + i]
            w_ref[i] = w_ref[i] + (real * rr - imag * ri)
            w_ref[12 + i] = w_ref[12 + i] + (real * ri + imag * rr)
            rho_ref[i] = rr - (real * ar - imag * ai)
            rho_ref[12 + i] = ri - (real * ai + imag * ar)
            if again is not None:
                br, bi = again[i // 3][i % 3]
                applied_ref[i] = ar - (real * br - imag * bi)
                applied_ref[12 + i] = ai - (real * bi + imag * br)

    def step(_, carry):
        applied = load_spinor(applied_ref)
        weight = weights(applied, load_spinor(rho_ref))
        advance(weight, apply(applied))
        return carry

    for i in range(24):
        w_ref[i] = jnp.zeros(TILE, F32)
    store_spinor(applied_ref, apply(load_spinor(rho_ref)))
    lax.fori_loop(0, NMR - 1, step, 0)
    advance(weights(load_spinor(applied_ref), load_spinor(rho_ref)), None)


def add_local_hops(total, half_w, link_to, link_from):
    lane = lane_ids()
    column = lane % 16

    def x_ahead(v):
        near = jnp.where(column == 7, lanes_by(v, -1), 0.0)
        return jnp.where(column == 15, lanes_by(v, 15), near)

    def x_behind(v):
        near = jnp.where(column == 8, lanes_by(v, 1), 0.0)
        return jnp.where(column == 0, lanes_by(v, -15), near)

    def y_ahead(v):
        return jnp.where(lane >= 112, lanes_by(v, -16), 0.0)

    def y_behind(v):
        return jnp.where(lane < 16, lanes_by(v, 16), 0.0)

    for direction, ahead, behind in ((X, x_ahead, x_behind), (Y, y_ahead, y_behind)):
        half = map_half(ahead, project(half_w, direction, -1))
        matrix = load_link(lambda i: link_to(direction, i))
        expand_into(total, color_apply(matrix, half, False), direction, -1)
        matrix = load_link(lambda i: link_from(direction, i))
        half = map_half(behind, color_apply(matrix, project(half_w, direction, 1), True))
        expand_into(total, half, direction, 1)


def outgoing(half_w, link_from, direction):
    matrix = load_link(lambda i: link_from(direction, i))
    ahead = color_apply(matrix, project(half_w, direction, 1), True)
    behind = project(half_w, direction, -1)
    return flat_half(ahead), flat_half(behind)


def store_pairs(even, ahead, behind, first_ref, second_ref):
    for i in range(len(ahead)):
        first_ref[i] = jnp.where(even, ahead[i], behind[i])
        second_ref[i] = jnp.where(even, behind[i], ahead[i])


def load_pairs(even, first, second):
    low = [jnp.where(even, b, a) for a, b in zip(first, second)]
    high = [jnp.where(even, a, b) for a, b in zip(first, second)]
    return low, high


def store_rows(ref, index, row):
    ref[index : index + 1, :] = row


def row_at(ref, time):
    here = time_ids() == time
    return unflat_half(
        [jnp.where(here, jnp.broadcast_to(ref[i : i + 1, :], TILE), 0.0) for i in range(12)]
    )


def store_faces(half_w, depth_half_w, link_from, t_refs, z_refs):
    ahead, behind = outgoing(depth_half_w, link_from, Z)
    store_pairs(is_even("gz"), ahead, behind, *z_refs)
    ahead, behind = outgoing(half_w, link_from, T)
    even = is_even("ta")[0:1, :]
    for i in range(12):
        low, high = behind[i][0:1, :], ahead[i][7:8, :]
        store_rows(t_refs[0], i, jnp.where(even, high, low))
        store_rows(t_refs[1], i, jnp.where(even, low, high))


def add_faces(total, link_to, t_refs, z_refs):
    low, high = load_pairs(
        is_even("gz"), [z_refs[0][i] for i in range(12)], [z_refs[1][i] for i in range(12)]
    )
    expand_into(total, unflat_half(low), Z, 1)
    matrix = load_link(lambda i: link_to(Z, i))
    expand_into(total, color_apply(matrix, unflat_half(high), False), Z, -1)
    time = time_ids()
    rows = [
        [jnp.broadcast_to(ref[i : i + 1, :], TILE) for i in range(12)] for ref in t_refs
    ]
    low, high = load_pairs(is_even("ta"), *rows)
    low = unflat_half([jnp.where(time == 0, v, 0.0) for v in low])
    high = unflat_half([jnp.where(time == 7, v, 0.0) for v in high])
    expand_into(total, low, T, 1)
    matrix = load_link(lambda i: link_to(T, i))
    expand_into(total, color_apply(matrix, high, False), T, -1)


def packed_lower(flat):
    low = time_ids() < 4
    return [jnp.where(low, flat[i + 6], times_by(flat[i], 4)) for i in range(6)]


def unpacked_lower(tiles):
    low = time_ids() < 4
    flat = [jnp.where(low, 0.0, v) for v in tiles]
    flat += [jnp.where(low, 0.0, times_by(v, 4)) for v in tiles]
    return unflat_half(flat)


def packed_split(flat):
    low = time_ids() < 4
    stay, move = [], []
    for i in range(6):
        turned = times_by(flat[i], 4)
        stay.append(jnp.where(low, turned, flat[i + 6]))
        move.append(jnp.where(low, flat[i + 6], turned))
    return stay, move


def join_split(low_tiles, high_tiles):
    low = time_ids() < 4
    flat = [jnp.where(low, a, b) for a, b in zip(low_tiles, high_tiles)]
    flat += [times_by(jnp.where(low, b, a), 4) for a, b in zip(low_tiles, high_tiles)]
    return unflat_half(flat)


def zero_spinor():
    zero = jnp.zeros(TILE, F32)
    return [[(zero, zero) for _ in range(3)] for _ in range(4)]


def masked_spinor(field, mask):
    return [[(jnp.where(mask, v[0], 0.0), jnp.where(mask, v[1], 0.0)) for v in row] for row in field]


def add_spinor(total, other):
    for s in range(4):
        for c in range(3):
            a, b = total[s][c], other[s][c]
            total[s][c] = (a[0] + b[0], a[1] + b[1])


def raw_links(links_ref):
    first = row_zero_first()
    return [
        lambda direction, i, color=color: compact(links_ref, direction * 18 + i, color, first)
        for color in range(2)
    ]


def fill_moved_links(moved_ref, links_ref, received_ref):
    first = row_zero_first()
    low = time_ids() < 4
    for i in range(72):
        zero = times_by(compact(links_ref, i, 0, first), 4)
        one = times_by(compact(links_ref, i, 1, first), 4)
        other = received_ref[i]
        moved_ref[i] = jnp.where(low, other, zero)
        moved_ref[72 + i] = jnp.where(low, times_by(other, 4), one)


def moved_links(moved_ref):
    return [
        lambda direction, i, color=color: moved_ref[72 * color + direction * 18 + i]
        for color in range(2)
    ]


def packed_upper(ref):
    low = time_ids() < 4
    return [jnp.where(low, times_by(ref[i], 4), ref[12 + i]) for i in range(12)]


def unpacked_upper(ref, base):
    return [ref[base + i] for i in range(12)] + [times_by(ref[base + i], 4) for i in range(12)]


def kernel_one(links_hbm, source_hbm, w_ref, rho_ref, other_ref, t0_ref, t1_ref, z0_ref, z1_ref,
               packed_ref, links_ref, applied_ref, masked_ref, source_ref, arrived):
    first = row_zero_first()
    link = raw_links(links_ref)
    copies = [
        pltpu.make_async_copy(
            links_hbm.at[direction * 18 : direction * 18 + 18],
            links_ref.at[direction * 18 : direction * 18 + 18],
            arrived.at[direction],
        )
        for direction in range(4)
    ]
    source_copy = pltpu.make_async_copy(source_hbm, source_ref, arrived.at[4])
    source_copy.start()
    for direction in (X, Y, T, Z):
        copies[direction].start()
    source_copy.wait()
    for i in range(24):
        rho_ref[i] = compact(source_ref, i, 0, first)
        other_ref[i] = compact(source_ref, i, 1, first)
    for direction in (X, Y, T):
        copies[direction].wait()
    solve(rho_ref, w_ref, applied_ref, masked_ref, link[0])
    copies[Z].wait()
    half_w = scaled(load_spinor(w_ref), 0.5)
    store_faces(half_w, half_w, link[0], (t0_ref, t1_ref), (z0_ref, z1_ref))
    total = load_spinor(other_ref)
    add_local_hops(total, half_w, link[1], link[0])
    store_spinor(other_ref, total)
    low = time_ids() < 4
    for i in range(72):
        zero = compact(links_ref, i, 0, first)
        one = compact(links_ref, i, 1, first)
        packed_ref[i] = jnp.where(low, times_by(one, 4), zero)
    for i, tile in enumerate(packed_upper(rho_ref)):
        packed_ref[72 + i] = tile


def kernel_two(links_ref, rho_in, other_in, t0_in, t1_in, z0_in, z1_in,
               w_ref, rest_ref, rho_ref, send_ref, tb_ref, z0_ref, z1_ref,
               applied_ref, masked_ref):
    link = raw_links(links_ref)
    total = load_spinor(other_in)
    add_faces(total, link[1], (t0_in, t1_in), (z0_in, z1_in))
    store_spinor(rho_ref, total)
    solve(rho_ref, w_ref, applied_ref, masked_ref, link[1])
    half_w = scaled(load_spinor(w_ref), 0.5)
    ahead, behind = outgoing(half_w, link[1], Z)
    store_pairs(is_even("gz"), packed_lower(ahead), packed_lower(behind), z0_ref, z1_ref)
    behind = flat_half(project(half_w, T, -1))
    for i in range(12):
        store_rows(tb_ref, i, behind[i][0:1, :])
    total = load_spinor(rho_in)
    add_local_hops(total, half_w, link[0], link[1])
    store_spinor(rest_ref, total)
    for i, tile in enumerate(packed_upper(rho_ref) + packed_upper(w_ref)):
        send_ref[i] = tile


def kernel_three(links_ref, moved_in, rest_in, rho_in, tb_in, received, z0_in, z1_in,
                 w_ref, rho_ref, other_ref, t0_ref, t1_ref, z0_ref, z1_ref, moved_ref,
                 applied_ref, masked_ref):
    fill_moved_links(moved_ref, links_ref, moved_in)
    link = moved_links(moved_ref)
    time = time_ids()
    low = time < 4
    ones, zeros = unpacked_upper(received, 0), unpacked_upper(moved_in, 72)
    for i in range(24):
        rho_ref[i] = jnp.where(low, ones[i], times_by(rest_in[i], 4))
        other_ref[i] = jnp.where(low, zeros[i], times_by(rho_in[i], 4))
    came = [jnp.where(low, 0.5 * v, 0.0) for v in unpacked_upper(received, 12)]
    came = [[(came[s * 3 + c], came[12 + s * 3 + c]) for c in range(3)] for s in range(4)]
    total = load_spinor(rho_ref)
    lower, higher = load_pairs(
        is_even("gz"), [z0_in[i] for i in range(6)], [z1_in[i] for i in range(6)]
    )
    expand_into(total, unpacked_lower(lower), Z, 1)
    matrix = load_link(lambda i: link[0](Z, i))
    expand_into(total, color_apply(matrix, unpacked_lower(higher), False), Z, -1)
    matrix = load_link(lambda i: link[0](T, i))
    half = color_apply(matrix, project(came, T, 1), True)
    half = map_half(lambda v: jnp.where(time == 4, times_by(v, 1), 0.0), half)
    expand_into(total, half, T, 1)
    store_spinor(rho_ref, total)
    total = load_spinor(other_ref)
    matrix = load_link(lambda i: link[1](T, i))
    expand_into(total, color_apply(matrix, row_at(tb_in, 3), False), T, -1)
    store_spinor(other_ref, total)
    solve(rho_ref, w_ref, applied_ref, masked_ref, link[0])
    half_w = scaled(load_spinor(w_ref), 0.5)
    depth_half_w = came
    add_spinor(depth_half_w, half_w)
    store_faces(half_w, depth_half_w, link[0], (t0_ref, t1_ref), (z0_ref, z1_ref))
    total = load_spinor(other_ref)
    add_local_hops(total, depth_half_w, link[1], link[0])
    store_spinor(other_ref, total)


def kernel_four(moved_ref, w_in, rho_in, other_in, t0_in, t1_in, z0_in, z1_in,
                w_ref, rest_ref, rho_ref, send_ref, ta_ref, z0_ref, z1_ref, za_ref, zb_ref,
                applied_ref, masked_ref):
    link = moved_links(moved_ref)
    total = load_spinor(other_in)
    add_faces(total, link[1], (t0_in, t1_in), (z0_in, z1_in))
    store_spinor(rho_ref, total)
    solve(rho_ref, w_ref, applied_ref, masked_ref, link[1])
    half_w = scaled(load_spinor(w_ref), 0.5)
    ahead, behind = outgoing(half_w, link[1], Z)
    ahead, ahead_move = packed_split(ahead)
    behind, behind_move = packed_split(behind)
    store_pairs(is_even("gz"), ahead, behind, z0_ref, z1_ref)
    for i in range(6):
        za_ref[i] = ahead_move[i]
        zb_ref[i] = behind_move[i]
    matrix = load_link(lambda i: link[1](T, i))
    ahead = flat_half(color_apply(matrix, project(half_w, T, 1), True))
    for i in range(12):
        store_rows(ta_ref, i, ahead[i][7:8, :])
    total = load_spinor(rho_in)
    add_local_hops(total, half_w, link[0], link[1])
    store_spinor(rest_ref, total)
    low = time_ids() < 4
    for i in range(24):
        send_ref[i] = jnp.where(low, rho_ref[i], times_by(rest_ref[i], 4))
        send_ref[24 + i] = jnp.where(low, w_ref[i], times_by(w_in[i], 4))


def kernel_five(links_ref, w0_ref, w1_ref, x0_ref, x1_ref, rest_in, rho_in, ta_in, received,
                z0_in, z1_in, za_in, zb_in, solution_ref, residual_ref):
    link = raw_links(links_ref)
    first = row_zero_first()
    time = time_ids()
    low = time < 4

    def put(ref, i, zero, one):
        ref[i, :, 0:128] = jnp.where(first, zero, one)
        ref[i, :, 128:256] = jnp.where(first, one, zero)

    update = []
    for i in range(24):
        other = received[24 + i]
        zero = jnp.where(low, times_by(x0_ref[i], 4), times_by(other, 4))
        one = jnp.where(low, times_by(x1_ref[i], 4), other)
        put(solution_ref, i, w0_ref[i] + zero, w1_ref[i] + one)
        update.append(zero)
    lower, higher = load_pairs(
        is_even("gz"), [z0_in[i] for i in range(6)], [z1_in[i] for i in range(6)]
    )
    faces = zero_spinor()
    expand_into(faces, join_split(lower, [za_in[i] for i in range(6)]), Z, 1)
    matrix = load_link(lambda i: jnp.where(low, link[0](Z, i), link[1](Z, i)))
    half = join_split(higher, [zb_in[i] for i in range(6)])
    expand_into(faces, color_apply(matrix, half, False), Z, -1)
    zero, one = masked_spinor(faces, low), masked_spinor(faces, jnp.logical_not(low))
    update = [
        [(0.5 * update[s * 3 + c], 0.5 * update[12 + s * 3 + c]) for c in range(3)] for s in range(4)
    ]
    half = map_half(
        lambda v: jnp.where(time == 3, times_by(v, -1), 0.0), project(update, T, -1)
    )
    matrix = load_link(lambda i: link[0](T, i))
    expand_into(zero, color_apply(matrix, half, False), T, -1)
    expand_into(one, row_at(ta_in, 4), T, 1)
    for s in range(4):
        for c in range(3):
            for part in range(2):
                i = part * 12 + s * 3 + c
                other = received[i]
                base_zero = jnp.where(low, times_by(rest_in[i], 4), times_by(other, 4))
                base_one = jnp.where(low, times_by(rho_in[i], 4), other)
                put(residual_ref, i, base_zero + zero[s][c][part], base_one + one[s][c][part])


def call(kernel, shapes, operands, solver=False, fetch=False, cost=3000000):
    scratch = []
    if solver:
        scratch = [pltpu.VMEM((24,) + TILE, F32), pltpu.VMEM((54,) + TILE, F32)]
    if fetch:
        operands = [pltpu.with_memory_space_constraint(v, pltpu.HBM) for v in operands]
        scratch.append(pltpu.VMEM((24, 8, 256), F32))
        scratch.append(pltpu.SemaphoreType.DMA((5,)))
    vmem = pl.BlockSpec(memory_space=pltpu.VMEM)
    place = pl.BlockSpec(memory_space=pltpu.HBM) if fetch else vmem
    return pl.pallas_call(
        kernel,
        out_shape=[jax.ShapeDtypeStruct(shape, F32) for shape in shapes],
        in_specs=[place] * len(operands),
        out_specs=[vmem] * len(shapes),
        scratch_shapes=scratch,
        compiler_params=pltpu.CompilerParams(vmem_limit_bytes=12 << 20),
        cost_estimate=pl.CostEstimate(flops=cost, bytes_accessed=cost // 2, transcendentals=0),
    )(*operands)


def moved_to(value, time_steps, depth_steps):
    times, depths = lax.axis_size("ta"), lax.axis_size("gz")
    if depth_steps == 0:
        return lax.ppermute(value, "ta", [(i, (i + time_steps) % times) for i in range(times)])
    pairs = [
        (t * depths + g, (t + time_steps) % times * depths + (g + depth_steps) % depths)
        for t in range(times)
        for g in range(depths)
    ]
    return lax.ppermute(value, ("ta", "gz"), pairs)


def exchanged(value, axis, odd):
    count = lax.axis_size(axis)
    pairs = [(i, (i + (1 if i % 2 == odd else -1)) % count) for i in range(count)]
    return lax.ppermute(value, axis, pairs)


def exchange_faces(t0, t1, z0, z1):
    z0 = exchanged(z0, "gz", 0)
    t0 = exchanged(t0, "ta", 0)
    z1 = exchanged(z1, "gz", 1)
    t1 = exchanged(t1, "ta", 1)
    return [t0, t1, z0, z1]


def per_device(links, source):
    links = links.reshape((72, 8, 256))
    source = source.reshape((24, 8, 256))
    spinor, half, quarter, rows = (24,) + TILE, (12,) + TILE, (6,) + TILE, (12, 128)
    faces = [rows] * 2 + [half] * 2
    w0, rho0, other, *sent, packed, links = call(
        kernel_one,
        [spinor] * 3 + faces + [(84,) + TILE, (72, 8, 256)],
        [links, source],
        solver=True,
        fetch=True,
    )
    moved = moved_to(packed, 1, 0)
    came = exchange_faces(*sent)
    w1, rest, rho1, send, tb, z0, z1 = call(
        kernel_two,
        [spinor] * 3 + [(24,) + TILE, rows, quarter, quarter],
        [links, rho0, other] + came,
        solver=True,
    )
    z0 = exchanged(z0, "gz", 0)
    z1 = exchanged(z1, "gz", 1)
    send = moved_to(send, 1, 0)
    x0, rho0, other, *sent, moved = call(
        kernel_three,
        [spinor] * 3 + faces + [(144,) + TILE],
        [links, moved, rest, rho1, tb, send, z0, z1],
        solver=True,
    )
    came = exchange_faces(*sent)
    x1, rest, rho1, send, ta, z0, z1, za, zb = call(
        kernel_four,
        [spinor] * 3 + [(48,) + TILE, rows] + [quarter] * 4,
        [moved, x0, rho0, other] + came,
        solver=True,
    )
    z0 = exchanged(z0, "gz", 0)
    z1 = exchanged(z1, "gz", 1)
    send = moved_to(send, -1, 0)
    za = moved_to(za, -1, 1)
    zb = moved_to(zb, -1, -1)
    solution, residual = call(
        kernel_five,
        [(24, 8, 256)] * 2,
        [links, w0, w1, x0, x1, rest, rho1, ta, send, z0, z1, za, zb],
    )
    return solution.reshape((24, 1, 8, 256)), residual.reshape((24, 1, 8, 256))


def solution(mesh):
    in_specs = (P(None, None, "gz", "ta", None), P(None, "gz", "ta", None))
    out_specs = (P(None, "gz", "ta", None), P(None, "gz", "ta", None))
    return jax.shard_map(
        per_device, mesh=mesh, in_specs=in_specs, out_specs=out_specs, check_vma=False
    )
```
